256 devices in a mesh: seq: 32 (over z, y), head: 8 (over x, core).
Axes of the slice: x: 4, y: 4, z: 8, core: 2. Of those that a mesh axis runs over, the one named last changes fastest.
Arguments:
- queries: bfloat16 [4096, 8192], P('seq', 'head'), may hold values from -6 to 6
- key_vectors: bfloat16 [4096, 8192], P('seq', 'head'), may hold values from -6 to 6
- value_vectors: bfloat16 [4096, 8192], P('seq', 'head'), may hold values from -6 to 6
- log_decay: float32 [4096, 64], P('seq', 'head'), may hold values from -2 to 0
- doc_ids: int32 [4096], P('seq'), may hold values from 0 to 3, as said below
- head_gain: float32 [8192], P('head'), may hold values from 0.4 to 1.6
- output_weight: bfloat16 [8192, 3072], P('head', 'seq'), may hold values from -0.0625 to 0.0625
- residual: bfloat16 [4096, 3072], P('seq', 'head'), may hold values from -8 to 8
- norm_gain: float32 [3072], replicated, may hold values from 0.4 to 1.6
- routing: int32 [4096, 2], P('seq'), may hold values from 0 to 31, all different within a row; in each aligned block of 128 rows (0 to 127, 128 to 255, ...) at most 16 rows name the same one
- route_weights: float32 [4096, 2], P('seq'), may hold values from 0.1 to 1
- gate_weight: bfloat16 [32, 3072, 4608], P('seq', None, 'head'), may hold values from -0.109375 to 0.109375
- up_weight: bfloat16 [32, 3072, 4608], P('seq', None, 'head'), may hold values from -0.109375 to 0.109375
- down_weight: bfloat16 [32, 4608, 3072], P('seq', 'head'), may hold values from -0.09375 to 0.09375
Outputs:
- mixed: bfloat16 [4096, 3072], P('seq', 'head')
The draws below stay inside these ranges and needn't reach their ends.
Inputs may be any that keep to these rules, and one draw needn't show every extreme that they name: `doc_ids`: ids never fall along the sequence and rise by one where a document starts; every id occurs. `routing`: the two experts of a position differ; among the rows of one index of seq no expert is named more than 16 times.
All inputs are finite; a program needn't handle non-finite values.
Results may differ from the reference program's by a relative error of at most 0.014.
Values may be sent and summed in bfloat16 or wider, within the bound.
A program may use at most 128 MiB of HBM per device.

```python
import math
import jax
import jax.numpy as jnp
import numpy as np
from jax import lax

D = 3072
HEADS = 64
HD = 128
FFW = 4608
NDOCS = 4
TOK_DEV = 128
EXPERTS = 32
SEQUENCE_SLOTS = 4096
CAP = 16
N_SEQ = 32
N_HEAD = 8


def draw_log_decay(key, part):
    stochastic_subseeds = jax.random.split(jax.random.fold_in(key, 11), 7)
    slow_share = 0.5
    slow_heads = jax.random.uniform(stochastic_subseeds[0], (HEADS,)) < slow_share
    slow_rate = jnp.log(10.0) * jax.random.uniform(stochastic_subseeds[1], (HEADS,), minval=0.1, maxval=0.4) / SEQUENCE_SLOTS
    fast_rate = jnp.log(10.0) / jax.random.uniform(stochastic_subseeds[2], (HEADS,), minval=30.0, maxval=50.0)
    fading_rate = jnp.where(slow_heads, slow_rate, fast_rate)
    noise_magnitude = jax.random.uniform(stochastic_subseeds[3], (SEQUENCE_SLOTS, HEADS), minval=0.5, maxval=1.5)
    block_factor = jnp.exp(jax.random.uniform(stochastic_subseeds[4], (SEQUENCE_SLOTS // TOK_DEV, 1), minval=jnp.log(0.5), maxval=jnp.log(2.0)))
    tile_multiplier = jnp.repeat(block_factor, TOK_DEV, axis=0)
    spike_locations = jax.random.randint(stochastic_subseeds[5], (2,), 0, SEQUENCE_SLOTS)
    objective_entries = jnp.log(jax.random.uniform(stochastic_subseeds[6], (2, 1), minval=0.5, maxval=0.8))
    spike_log_height = jnp.zeros((SEQUENCE_SLOTS, 1), jnp.float32).at[spike_locations].add(objective_entries)
    return (-fading_rate[None, :] * noise_magnitude * tile_multiplier + spike_log_height).astype(jnp.float32)


def draw_doc_ids(key, part):
    shuffled = jax.random.permutation(jax.random.fold_in(key, 37), SEQUENCE_SLOTS - 1)
    starts = (shuffled[:NDOCS - 1] + 1).astype(jnp.int32)
    position = jnp.arange(SEQUENCE_SLOTS, dtype=jnp.int32)
    return jnp.sum((position[:, None] >= starts[None, :]).astype(jnp.int32), axis=1).astype(jnp.int32)


def draw_residual(key, part):
    stochastic_subseeds = jax.random.split(jax.random.fold_in(key, 23), 2)
    base_draw = jax.random.normal(stochastic_subseeds[0], (SEQUENCE_SLOTS, D), jnp.float32)
    noise_magnitude = jnp.exp(jax.random.uniform(stochastic_subseeds[1], (1, D), minval=jnp.log(0.5), maxval=jnp.log(2.0)))
    ramp_scale = 0.6 + 1.2 * jnp.arange(D, dtype=jnp.float32)[None, :] / D
    return jnp.clip(base_draw * noise_magnitude * ramp_scale, -8.0, 8.0).astype(jnp.bfloat16)


def block_scale(key, dims, pieces, least, high):
    level, own = 1.0, jax.random.fold_in(key, 6)
    for dim, shards_of in pieces:
        steps = jnp.exp(jax.random.uniform(jax.random.fold_in(own, dim), (shards_of,), jnp.float32, least / len(pieces), high / len(pieces)))
        level = level * jnp.repeat(steps, dims[dim] // shards_of).reshape([-1 if axis == dim else 1 for axis in range(len(dims))])
    return level


def routed_block(key, own, number, rows, count, top, limit, lean):
    ranking = jax.random.permutation(key, count)
    packed, common = portions_of(count, rows * top, limit, lean, True), portions_of(count, rows * top, limit, lean, False)
    places = jnp.arange(count)

    def named(sizes, rotation):
        used = int((sizes > 0).sum())
        fixed = max(1, used // 4)
        shifted = fixed + (places - fixed + rotation * (used - fixed)) % max(1, count - fixed)
        return jnp.zeros((count,), jnp.int32).at[ranking[jnp.where(places < fixed, places, shifted)]].set(jnp.asarray(sizes, jnp.int32))

    sizes = jnp.where(number % 4 == 0, named(packed, number // 4), named(common, number - number // 4 - 1))
    mixed = jax.random.permutation(jax.random.fold_in(own, 3), count)
    source_of, sink = mixed[0:count // 2 * 2:2], mixed[1:count // 2 * 2:2]
    slack = jnp.minimum(sizes[source_of] - 1, limit - sizes[sink]) // 2
    slack = jnp.where((source_of == ranking[0]) | (sink == ranking[0]) | (sizes[sink] == 0), 0, jnp.maximum(slack, 0))
    shifted = jax.random.randint(jax.random.fold_in(own, 4), (count // 2,), 0, 1 << 20) % (slack + 1)
    sizes = sizes.at[source_of].add(-shifted).at[sink].add(shifted)
    labels = jnp.searchsorted(jnp.cumsum(sizes), jnp.arange(rows * top), side="right").astype(jnp.int32)
    grid = labels.reshape(top, rows).T
    grid = grid[jax.random.permutation(jax.random.fold_in(own, 1), rows)]
    rotation = jax.random.randint(jax.random.fold_in(own, 2), (rows, 1), 0, top)
    return jnp.take_along_axis(grid, (jnp.arange(top)[None, :] + rotation) % top, axis=1)


def portions_of(number_of, total, bound, lean, full):
    portions = [(1 << 20) // math.isqrt(standing ** lean) + 1 for standing in range(1, number_of + 1)]
    largest = bound if full else min(bound, max(-(-total // number_of), total * portions[0] // sum(portions)))
    least = 1 if total - largest >= number_of - 1 else 0
    counts, surplus = [largest] + [least] * (number_of - 1), total - largest - least * (number_of - 1)
    while surplus > 0:
        movable = [i for i in range(1, number_of) if counts[i] < largest] or [i for i in range(1, number_of) if counts[i] < bound]
        whole, left = sum([portions[i] for i in movable]), surplus
        for i in movable:
            more = min(bound - counts[i], max(1, left * portions[i] // whole), surplus)
            counts[i] = counts[i] + more
            surplus = surplus - more
    return np.array(counts)


def gaussian(stream_key, shape, width, most, shards=(), held_as=jnp.bfloat16):
    array = width * jax.random.normal(stream_key, shape, jnp.float32)
    if shards:
        array = array * block_scale(stream_key, shape, shards, -0.22, 0.18)
    return jnp.clip(array, -most, most).astype(held_as)


def setup_inputs(seed: int = 0) -> dict:
    key_of = jax.random.split(jax.random.key(seed), 15)
    queries = gaussian(key_of[0], (SEQUENCE_SLOTS, HEADS * HD), 1.0, 6.0, ((0, 32), (1, 8)))
    key_vectors = gaussian(key_of[1], (SEQUENCE_SLOTS, HEADS * HD), 1.0, 6.0, ((0, 32), (1, 8)))
    value_vectors = gaussian(key_of[2], (SEQUENCE_SLOTS, HEADS * HD), 1.0, 6.0, ((0, 32), (1, 8)))
    log_decay = draw_log_decay(jax.random.fold_in(key_of[14], 71), 0)
    doc_ids = draw_doc_ids(jax.random.fold_in(key_of[14], 71), 0)
    head_gain = jnp.clip(1.0 + 0.12 * jax.random.normal(key_of[5], (HEADS * HD,), jnp.float32), 0.4, 1.6)
    output_weight = gaussian(key_of[6], (HEADS * HD, D), (HEADS * HD) ** -0.5, 0.0625, ((0, 8), (1, 32)))
    residual = draw_residual(jax.random.fold_in(key_of[14], 71), 0)
    norm_gain = jnp.clip(1.0 + 0.12 * jax.random.normal(key_of[8], (D,), jnp.float32), 0.4, 1.6)
    routing_keys = jax.random.split(jax.random.fold_in(key_of[9], 1), SEQUENCE_SLOTS // TOK_DEV)
    routing_turns = jax.random.permutation(jax.random.fold_in(key_of[9], 3), SEQUENCE_SLOTS // TOK_DEV)
    routing = jax.vmap(lambda own, number: routed_block(jax.random.fold_in(key_of[9], 2), own, number, TOK_DEV, EXPERTS, 2, CAP, 2))(routing_keys, routing_turns).reshape((SEQUENCE_SLOTS, 2))
    route_weights = jnp.clip(0.1 + 0.9 * jax.random.uniform(key_of[10], (SEQUENCE_SLOTS, 2), jnp.float32) ** block_scale(key_of[10], (SEQUENCE_SLOTS, 2), ((0, 32),), -0.2, 0.2), 0.1, 1.0)
    gate_weight = gaussian(key_of[11], (EXPERTS, D, FFW), D ** -0.5, 0.109375, ((0, 32), (2, 8)))
    up_weight = gaussian(key_of[12], (EXPERTS, D, FFW), D ** -0.5, 0.109375, ((0, 32), (2, 8)))
    down_weight = gaussian(key_of[13], (EXPERTS, FFW, D), FFW ** -0.5, 0.09375, ((0, 32), (1, 8)))
    return {"queries": queries, "key_vectors": key_vectors, "value_vectors": value_vectors, "log_decay": log_decay, "doc_ids": doc_ids, "head_gain": head_gain, "output_weight": output_weight, "residual": residual, "norm_gain": norm_gain, "routing": routing, "route_weights": route_weights, "gate_weight": gate_weight, "up_weight": up_weight, "down_weight": down_weight}


EPSILON = 1e-06
FULL_PRECISION = lax.Precision.HIGHEST

def reference(queries, key_vectors, value_vectors, log_decay, doc_ids, head_gain, output_weight, residual, norm_gain, routing, route_weights, gate_weight, up_weight, down_weight):
    blocks = SEQUENCE_SLOTS // TOK_DEV
    query_blocks = queries.reshape(blocks, TOK_DEV, HEADS, HD)
    key_blocks = key_vectors.reshape(blocks, TOK_DEV, HEADS, HD)
    value_blocks = value_vectors.reshape(blocks, TOK_DEV, HEADS, HD)
    decay_blocks = log_decay.reshape(blocks, TOK_DEV, HEADS)
    doc_blocks = doc_ids.reshape(blocks, TOK_DEV)

    def advance(carry_pair, block_data):
        carried, last_doc = carry_pair
        query_heads, key_heads, value_heads, decay_log, doc_block = block_data
        decay_sum = jnp.cumsum(decay_log, axis=0)
        decay_rows = decay_sum.T
        gap_matrix = decay_rows[:, :, None] - decay_rows[:, None, :]
        row_index = lax.broadcasted_iota(jnp.int32, (TOK_DEV, TOK_DEV), 0)
        col_index = lax.broadcasted_iota(jnp.int32, (TOK_DEV, TOK_DEV), 1)
        kept_mask = (col_index <= row_index) & (doc_block[:, None] == doc_block[None, :])
        decay_matrix = jnp.where(kept_mask[None], jnp.exp(jnp.minimum(gap_matrix, 0.0)), 0.0)
        scores = jnp.einsum('thd,shd->hts', query_heads.astype(jnp.float32), key_heads.astype(jnp.float32), precision=FULL_PRECISION)
        weighted = (scores * decay_matrix).astype(jnp.bfloat16)
        inside = jnp.einsum('hts,shd->thd', weighted.astype(jnp.float32), value_heads.astype(jnp.float32), precision=FULL_PRECISION)
        doc_float = doc_block.astype(jnp.float32)
        reach_gain = jnp.exp(decay_sum) * (doc_float == last_doc).astype(jnp.float32)[:, None]
        outside = jnp.einsum('thd,hde->the', query_heads.astype(jnp.float32), carried, precision=FULL_PRECISION) * reach_gain[:, :, None]
        tail_gain = jnp.exp(decay_sum[-1][None, :] - decay_sum) * (doc_block == doc_block[-1]).astype(jnp.float32)[:, None]
        own_state = jnp.einsum('thd,the->hde', key_heads.astype(jnp.float32) * tail_gain[:, :, None], value_heads.astype(jnp.float32), precision=FULL_PRECISION)
        through = jnp.exp(decay_sum[-1]) * ((doc_block[0] == doc_block[-1]) & (doc_float[0] == last_doc)).astype(jnp.float32)
        new_state = through[:, None, None] * carried + own_state
        return ((new_state, doc_float[-1]), inside + outside)
    start_pair = (jnp.zeros((HEADS, HD, HD), jnp.float32), jnp.asarray(-1.0, dtype=jnp.float32))
    _, heads_raw = lax.scan(advance, start_pair, (query_blocks, key_blocks, value_blocks, decay_blocks, doc_blocks))
    heads_raw = heads_raw.reshape(SEQUENCE_SLOTS, HEADS, HD)
    inv_norm = lax.rsqrt(lax.optimization_barrier(jnp.mean(heads_raw * heads_raw, axis=2, keepdims=True)) + EPSILON)
    attended = ((heads_raw * inv_norm).reshape(SEQUENCE_SLOTS, HEADS * HD) * head_gain).astype(jnp.bfloat16)
    projected = jnp.dot(attended, output_weight, preferred_element_type=jnp.float32)
    middle = lax.optimization_barrier((residual.astype(jnp.float32) + projected).astype(jnp.bfloat16))
    middle_float = middle.astype(jnp.float32)
    row_norm = lax.rsqrt(lax.optimization_barrier(jnp.mean(middle_float * middle_float, axis=1, keepdims=True)) + EPSILON)
    normed = (middle_float * row_norm * norm_gain).astype(jnp.bfloat16)
    capacity = N_SEQ * CAP
    flat_ids = routing.reshape(-1)
    hit_table = (flat_ids[:, None] == jnp.arange(EXPERTS, dtype=jnp.int32)[None, :]).astype(jnp.int32)
    slot_rank = lax.optimization_barrier(jnp.sum((jnp.cumsum(hit_table, axis=0) - 1) * hit_table, axis=1)).astype(jnp.int32)
    slot_place = (flat_ids * capacity + slot_rank).astype(jnp.int32)
    owner_row = (jnp.arange(2 * SEQUENCE_SLOTS, dtype=jnp.int32) // 2).astype(jnp.int32)
    slot_table = jnp.full((EXPERTS * capacity,), SEQUENCE_SLOTS, jnp.int32).at[slot_place].set(owner_row)
    padded = jnp.concatenate([normed, jnp.zeros((1, D), jnp.bfloat16)], axis=0)
    group_size = FFW // N_HEAD

    def serve(inputs):
        slot_rows, gate_matrix, up_matrix, down_matrix = inputs
        row_block = padded[slot_rows]
        accumulated = jnp.zeros((slot_rows.shape[0], D), jnp.float32)
        for part_index in range(N_HEAD):
            group_start = part_index * group_size
            gate_proj = jnp.dot(row_block, gate_matrix[:, group_start:group_start + group_size], preferred_element_type=jnp.float32)
            up_proj = jnp.dot(row_block, up_matrix[:, group_start:group_start + group_size], preferred_element_type=jnp.float32)
            hidden = (jax.nn.silu(gate_proj) * up_proj).astype(jnp.bfloat16)
            piece_out = jnp.dot(hidden, down_matrix[group_start:group_start + group_size], preferred_element_type=jnp.float32)
            accumulated = accumulated + piece_out.astype(jnp.bfloat16).astype(jnp.float32)
        return accumulated
    served = lax.map(serve, (slot_table.reshape(EXPERTS, capacity), gate_weight, up_weight, down_weight))
    picked = served.reshape(EXPERTS * capacity, D)[slot_place]
    expert_sum = lax.optimization_barrier(jnp.sum(picked.reshape(SEQUENCE_SLOTS, 2, D) * route_weights[:, :, None], axis=1))
    return (middle_float + expert_sum).astype(jnp.bfloat16)
```

```python
import functools

import jax
import jax.numpy as jnp
from jax import lax
from jax.experimental import pallas as pl
from jax.experimental.pallas import tpu as pltpu
from jax.sharding import PartitionSpec as P

MESH = pl.DeviceIdType.MESH
F32, BF16 = jnp.float32, jnp.bfloat16
EPSILON = 1e-06
NZ, NY, NX = 8, 4, 4
NSEQ, NHEAD = NZ * NY, 2 * NX
TOK, HEADS, HD = 128, 8, 128
WCOLS = 96
PART = 384
D = PART * NHEAD
CAP = 16
NG = 4
GSRC = NSEQ // NG
GROWS = GSRC * CAP
FF = 576
VMEM_LIMIT = 60 * 1024 * 1024


def nt(a, b):
    return lax.dot_general(a, b, (((1,), (1,)), ((), ())), preferred_element_type=F32)


def nn(a, b):
    return jnp.dot(a, b, preferred_element_type=F32)


def remote(src, dst, send_sem, recv_sem, **device):
    return pltpu.make_async_remote_copy(
        src_ref=src,
        dst_ref=dst,
        send_sem=send_sem,
        recv_sem=recv_sem,
        device_id=device,
        device_id_type=MESH,
    )


def greet(me, hd):
    barrier = pltpu.get_barrier_semaphore()

    @pl.loop(1, NSEQ)
    def _(d):
        pl.semaphore_signal(
            barrier, inc=1, device_id={"seq": lax.rem(me + d, NSEQ)}, device_id_type=MESH
        )

    @pl.loop(1, NHEAD)
    def _(d):
        pl.semaphore_signal(
            barrier, inc=1, device_id={"head": lax.rem(hd + d, NHEAD)}, device_id_type=MESH
        )

    return barrier


def columns(row):
    return jnp.transpose(jnp.broadcast_to(row, (TOK, TOK)))


def attention_kernel(
    q_ref,
    k_ref,
    v_ref,
    ld_ref,
    doc_ref,
    hg_ref,
    w_ref,
    res_ref,
    mid_ref,
    decay,
    own_state,
    own_info,
    all_state,
    all_info,
    own_carry,
    all_carry,
    inner,
    attended,
    weight,
    partial,
    arrived,
    column_out,
    column_in,
    s_state,
    r_state,
    s_info,
    r_info,
    s_carry,
    r_carry,
    s_att,
    r_att,
    s_w,
    r_w,
    s_part,
    r_part,
    s_col,
    r_col,
):
    me, hd = lax.axis_index("seq"), lax.axis_index("head")
    zi, yi = me // NY, lax.rem(me, NY)
    barrier = greet(me, hd)

    rows = lax.broadcasted_iota(jnp.int32, (TOK, TOK), 0)
    cols = lax.broadcasted_iota(jnp.int32, (TOK, TOK), 1)
    upper = (rows <= cols).astype(F32)
    sums = jnp.dot(
        ld_ref[...], upper, preferred_element_type=F32, precision=lax.Precision.HIGHEST
    )
    decay[...] = sums
    last = sums[:, TOK - 1 : TOK]
    doc = doc_ref[...].astype(F32)
    doc_first, doc_last = doc[:, 0:1], doc[:, TOK - 1 : TOK]
    tail = jnp.exp(last - sums) * (doc == doc_last).astype(F32)
    gain = jnp.exp(last) * (doc_first == doc_last).astype(F32)
    own_info[0:8, :] = jnp.broadcast_to(gain, (HEADS, TOK))
    own_info[8:16, :] = jnp.where(
        lax.broadcasted_iota(jnp.int32, (8, TOK), 0) == 0, doc_first, doc_last
    )
    for h in range(HEADS):
        lanes = slice(h * HD, (h + 1) * HD)
        key_t = jnp.transpose(k_ref[:, lanes].astype(F32))
        state = nn((key_t * tail[h : h + 1, :]).astype(BF16), v_ref[:, lanes])
        own_state[4 * h : 4 * h + 4] = state.astype(BF16).reshape(4, 32, HD)

    pl.semaphore_wait(barrier, NSEQ + NHEAD - 2)

    @pl.loop(1, NSEQ)
    def _(d):
        to = lax.rem(me + d, NSEQ)
        remote(own_info, all_info.at[me], s_info, r_info, seq=to).start()
        remote(own_state.at[to], all_state.at[me], s_state, r_state, seq=to).start()

    all_state[me] = own_state[me]
    all_info[me] = own_info[...]

    w_rows = pl.ds(pl.multiple_of(zi * WCOLS, 32), WCOLS)

    @pl.loop(1, NZ)
    def _(d):
        to = lax.rem(zi + d, NZ) * NY + yi
        remote(w_ref, weight.at[w_rows], s_w, r_w, seq=to).start()

    doc_rows = jnp.broadcast_to(doc, (TOK, TOK))
    kept = (cols <= rows) & (jnp.transpose(doc_rows) == doc_rows)
    for h in range(HEADS):
        lanes = slice(h * HD, (h + 1) * HD)
        decay_row = jnp.broadcast_to(decay[h : h + 1, :], (TOK, TOK))
        gap = jnp.transpose(decay_row) - decay_row
        factor = jnp.where(kept, jnp.exp(jnp.minimum(gap, 0.0)), 0.0)
        weighted = (nt(q_ref[:, lanes], k_ref[:, lanes]) * factor).astype(BF16)
        inner[:, lanes] = nn(weighted, v_ref[:, lanes])
    weight[w_rows, :] = w_ref[...]

    others = NSEQ - 1
    remote(
        own_state.at[0:others], all_state.at[0:others], s_state, r_state, seq=me
    ).wait_recv()
    remote(
        all_info.at[0:others], all_info.at[0:others], s_info, r_info, seq=me
    ).wait_recv()
    my_head = me // 4

    def scan(b, carry):
        carried, before = carry
        own_carry[b] = carried.astype(BF16)
        gain_row = all_info[b, pl.ds(my_head, 1), :]
        docs = all_info[b, 8:16, :]
        through = jnp.where(docs[0:1, :] == before, gain_row, 0.0)
        return all_state[b].astype(F32) + through * carried, docs[1:2, :]

    lax.fori_loop(
        0, NSEQ, scan, (jnp.zeros((32, HD), F32), jnp.full((1, HD), -1.0, F32))
    )

    @pl.loop(1, NSEQ)
    def _(d):
        to = lax.rem(me + d, NSEQ)
        remote(own_carry.at[to], all_carry.at[me], s_carry, r_carry, seq=to).start()

    all_carry[me] = own_carry[me]
    before_doc = all_info[jnp.maximum(me - 1, 0), 8:16, :][1:2, :]
    before_doc = jnp.where(jnp.full((1, TOK), me, jnp.int32) == 0, -1.0, before_doc)
    reach = jnp.exp(decay[...]) * (doc == before_doc).astype(F32)
    remote(
        own_carry.at[0:others], all_carry.at[0:others], s_carry, r_carry, seq=me
    ).wait_recv()
    for h in range(HEADS):
        lanes = slice(h * HD, (h + 1) * HD)
        carried = all_carry[4 * h : 4 * h + 4].reshape(HD, HD)
        raw = inner[:, lanes] + nn(q_ref[:, lanes], carried) * columns(reach[h : h + 1, :])
        scale = lax.rsqrt(jnp.mean(raw * raw, axis=1, keepdims=True) + EPSILON)
        attended[yi, :, lanes] = (raw * scale * hg_ref[:, lanes]).astype(BF16)
        if h % 2 == 1:
            pair = slice((h - 1) * HD, (h + 1) * HD)
            for d in range(1, NY):
                to = zi * NY + lax.rem(yi + d, NY)
                remote(
                    attended.at[yi, :, pair],
                    attended.at[yi, :, pair],
                    s_att,
                    r_att.at[yi],
                    seq=to,
                ).start()

    remote(
        weight.at[0 : (NZ - 1) * WCOLS], weight.at[0 : (NZ - 1) * WCOLS], s_w, r_w, seq=me
    ).wait_recv()

    @pl.loop(0, NY)
    def _(i):
        y = lax.rem(yi + NY - i, NY)

        @pl.when(i > 0)
        def _():
            remote(attended.at[y], attended.at[y], s_att, r_att.at[y], seq=me).wait_recv()

        partial[y] = nt(weight[...], attended[y]).astype(BF16)

        @pl.loop(1, NHEAD)
        def _(d):
            to = lax.rem(hd + d, NHEAD)
            remote(
                partial.at[y, pl.ds(pl.multiple_of(to * WCOLS, 32), WCOLS)],
                arrived.at[y, hd],
                s_part,
                r_part.at[y],
                head=to,
            ).start()

        arrived[y, hd] = partial[y, pl.ds(pl.multiple_of(hd * WCOLS, 32), WCOLS), :]

    @pl.loop(0, NY)
    def _(i):
        y = lax.rem(yi + NY - i, NY)
        remote(
            arrived.at[y, 0 : NHEAD - 1],
            arrived.at[y, 0 : NHEAD - 1],
            s_part,
            r_part.at[y],
            head=hd,
        ).wait_recv()
        total = arrived[y, 0].astype(F32)
        for h in range(1, NHEAD):
            total = total + arrived[y, h].astype(F32)
        column_out[y] = total.astype(BF16)

        @pl.when(i > 0)
        def _():
            remote(
                column_out.at[y], column_in.at[yi], s_col, r_col, seq=zi * NY + y
            ).start()

        @pl.when(i == 0)
        def _():
            column_in[yi] = total.astype(BF16)

    remote(
        column_in.at[0 : NY - 1], column_in.at[0 : NY - 1], s_col, r_col, seq=me
    ).wait_recv()
    for c in range(PART // HD):
        lanes = slice(c * HD, (c + 1) * HD)
        slab = column_in[...].astype(F32).reshape(PART, TOK)[c * HD : (c + 1) * HD, :]
        mid_ref[:, lanes] = (res_ref[:, lanes].astype(F32) + jnp.transpose(slab)).astype(BF16)

    remote(
        own_state.at[0:others], all_state.at[0:others], s_state, r_state, seq=me
    ).wait_send()
    remote(
        all_info.at[0:others], all_info.at[0:others], s_info, r_info, seq=me
    ).wait_send()
    remote(
        own_carry.at[0:others], all_carry.at[0:others], s_carry, r_carry, seq=me
    ).wait_send()
    remote(attended.at[0:3], attended.at[0:3], s_att, r_att.at[0], seq=me).wait_send()
    remote(
        weight.at[0 : (NZ - 1) * WCOLS], weight.at[0 : (NZ - 1) * WCOLS], s_w, r_w, seq=me
    ).wait_send()
    remote(
        arrived.at[:, 0 : NHEAD - 1],
        arrived.at[:, 0 : NHEAD - 1],
        s_part,
        r_part.at[0],
        head=hd,
    ).wait_send()
    remote(
        column_in.at[0 : NY - 1], column_in.at[0 : NY - 1], s_col, r_col, seq=me
    ).wait_send()


def attention(q, k, v, ld_t, doc, gain, w_t, residual):
    vmem = pl.BlockSpec(memory_space=pltpu.VMEM)
    dma = pltpu.SemaphoreType.DMA
    return pl.pallas_call(
        attention_kernel,
        out_shape=jax.ShapeDtypeStruct((TOK, PART), BF16),
        in_specs=[vmem] * 8,
        out_specs=vmem,
        scratch_shapes=[
            pltpu.VMEM((HEADS, TOK), F32),
            pltpu.VMEM((NSEQ, 32, HD), BF16),
            pltpu.VMEM((16, TOK), F32),
            pltpu.VMEM((NSEQ, 32, HD), BF16),
            pltpu.VMEM((NSEQ, 16, TOK), F32),
            pltpu.VMEM((NSEQ, 32, HD), BF16),
            pltpu.VMEM((NSEQ, 32, HD), BF16),
            pltpu.VMEM((TOK, HEADS * HD), F32),
            pltpu.VMEM((NY, TOK, HEADS * HD), BF16),
            pltpu.VMEM((NZ * WCOLS, HEADS * HD), BF16),
            pltpu.VMEM((NY, NZ * WCOLS, TOK), BF16),
            pltpu.VMEM((NY, NHEAD, WCOLS, TOK), BF16),
            pltpu.VMEM((NY, WCOLS, TOK), BF16),
            pltpu.VMEM((NY, WCOLS, TOK), BF16),
            dma,
            dma,
            dma,
            dma,
            dma,
            dma,
            dma,
            dma((NY,)),
            dma,
            dma,
            dma,
            dma((NY,)),
            dma,
            dma,
        ],
        compiler_params=pltpu.CompilerParams(
            collective_id=0, has_side_effects=True, vmem_limit_bytes=VMEM_LIMIT
        ),
        name="attention",
    )(q, k, v, ld_t, doc, gain, w_t, residual)


def expert_kernel(
    mid_ref,
    rout_ref,
    mix_ref,
    ng_ref,
    gate_hbm,
    up_hbm,
    down_hbm,
    out_ref,
    gate,
    up,
    down,
    outgoing,
    rows_in,
    normed,
    result,
    pair_in,
    pair_sum,
    plane_in,
    summed,
    returned,
    s_load,
    s_disp,
    r_disp,
    s_gath,
    r_gath,
    s_fwd,
    r_fwd,
    s_pair,
    r_pair,
    s_plane,
    r_plane,
    s_ret,
    r_ret,
):
    me, hd = lax.axis_index("seq"), lax.axis_index("head")
    xi, core = hd // 2, lax.rem(hd, 2)
    partner = xi * 2 + 1 - core
    group = me // GSRC
    barrier = greet(me, hd)
    loads = [
        pltpu.make_async_copy(gate_hbm, gate, s_load.at[0]),
        pltpu.make_async_copy(up_hbm, up, s_load.at[1]),
        pltpu.make_async_copy(down_hbm, down, s_load.at[2]),
    ]
    for load in loads:
        load.start()

    expert = lax.broadcasted_iota(jnp.int32, (NSEQ, TOK), 0)
    hits = [(expert == rout_ref[j : j + 1, :]).astype(F32) for j in range(2)]
    earlier = (
        lax.broadcasted_iota(jnp.int32, (TOK, TOK), 0)
        < lax.broadcasted_iota(jnp.int32, (TOK, TOK), 1)
    ).astype(BF16)
    count = nn((hits[0] + hits[1]).astype(BF16), earlier)
    places = [
        rout_ref[j : j + 1, :].astype(F32) * CAP
        + jnp.sum(hits[j] * count, axis=0, keepdims=True)
        for j in range(2)
    ]
    slot = lax.broadcasted_iota(jnp.int32, (NSEQ * CAP, TOK), 0).astype(F32)
    chosen = (slot == places[0]).astype(F32) + (slot == places[1]).astype(F32)
    outgoing[...] = (
        nn(chosen.astype(BF16), mid_ref[...]).astype(BF16).reshape(NSEQ, CAP, PART)
    )

    pl.semaphore_wait(barrier, NSEQ + NHEAD - 2)

    def my_rows(index):
        return pl.ds(pl.multiple_of(index * CAP, CAP), CAP)

    def group_rows(index):
        return pl.ds(pl.multiple_of(index * GROWS, GROWS), GROWS)

    @pl.loop(1, NSEQ)
    def _(d):
        to = lax.rem(me + d, NSEQ)
        remote(
            outgoing.at[to],
            rows_in.at[hd, my_rows(me)],
            s_disp,
            r_disp.at[group],
            seq=to,
        ).start()

    rows_in[hd, my_rows(me), :] = outgoing[me]

    def gather(i):
        g = lax.rem(group + NG - i, NG)
        part = group_rows(g)

        @pl.when(i == 0)
        def _():
            remote(
                outgoing.at[0 : GSRC - 1],
                outgoing.at[0 : GSRC - 1],
                s_disp,
                r_disp.at[g],
                seq=me,
            ).wait_recv()

        @pl.when(i > 0)
        def _():
            remote(
                outgoing.at[0:GSRC], outgoing.at[0:GSRC], s_disp, r_disp.at[g], seq=me
            ).wait_recv()

        for d in (2, 1, 3):
            to = lax.rem(xi + d, NX) * 2 + core
            remote(
                rows_in.at[hd, part],
                rows_in.at[hd, part],
                s_gath,
                r_gath.at[g, xi],
                head=to,
            ).start()
        remote(
            rows_in.at[hd, part], rows_in.at[hd, part], s_fwd, r_fwd.at[g], head=partner
        ).start()

    def forward(i):
        g = lax.rem(group + NG - i, NG)
        part = group_rows(g)
        for d in (1, 3, 2):
            x = lax.rem(xi + d, NX)
            block = rows_in.at[x * 2 + core, part]
            remote(block, block, s_gath, r_gath.at[g, x], head=hd).wait_recv()
            remote(block, block, s_fwd, r_fwd.at[g], head=partner).start()

    def serve(i):
        g = lax.rem(group + NG - i, NG)
        part = group_rows(g)

        @pl.when(i == 0)
        def _():
            for load in loads:
                load.wait()

        remote(
            rows_in.at[0:NX, 0:GROWS], rows_in.at[0:NX, 0:GROWS], s_fwd, r_fwd.at[g], head=hd
        ).wait_recv()
        squares = jnp.zeros((GROWS, HD), F32)
        for h in range(NHEAD):
            block = rows_in[h, part, :].astype(F32)
            block = block * block
            for c in range(PART // HD):
                squares = squares + block[:, c * HD : (c + 1) * HD]
        scale = lax.rsqrt(jnp.sum(squares, axis=1, keepdims=True) / D + EPSILON)
        for h in range(NHEAD):
            lanes = slice(h * PART, (h + 1) * PART)
            normed[:, lanes] = (
                rows_in[h, part, :].astype(F32) * scale * ng_ref[:, lanes]
            ).astype(BF16)
        gated = nt(normed[...], gate[...])
        upped = nt(normed[...], up[...])
        hidden = (gated / (1.0 + jnp.exp(-gated)) * upped).astype(BF16)
        for h in range(NHEAD):
            lanes = slice(h * PART, (h + 1) * PART)
            result[h % 2, h // 2, part, :] = nn(hidden, down[:, lanes]).astype(BF16)
        remote(
            result.at[1 - core, :, part],
            pair_in.at[:, part],
            s_pair,
            r_pair.at[g],
            head=partner,
        ).start()

    def reduce_pair(i):
        g = lax.rem(group + NG - i, NG)
        part = group_rows(g)
        remote(
            pair_in.at[:, part], pair_in.at[:, part], s_pair, r_pair.at[g], head=hd
        ).wait_recv()
        for d in (2, 1, 3, 0):
            x = lax.rem(xi + d, NX)
            pair_sum[x, part, :] = (
                result[core, x, part, :].astype(F32) + pair_in[x, part, :].astype(F32)
            ).astype(BF16)
            if d:
                remote(
                    pair_sum.at[x, part],
                    plane_in.at[xi, part],
                    s_plane,
                    r_plane.at[g],
                    head=x * 2 + core,
                ).start()

    def reduce_plane(i):
        g = lax.rem(group + NG - i, NG)
        part = group_rows(g)
        remote(
            plane_in.at[0 : NX - 1, part],
            plane_in.at[0 : NX - 1, part],
            s_plane,
            r_plane.at[g],
            head=hd,
        ).wait_recv()
        total = pair_sum[xi, part, :].astype(F32)
        for d in range(1, NX):
            total = total + plane_in[lax.rem(xi + d, NX), part, :].astype(F32)
        summed[part, :] = total.astype(BF16)

        @pl.loop(0, GSRC)
        def _(j):
            to = g * GSRC + j

            @pl.when(to != me)
            def _():
                remote(
                    summed.at[my_rows(to)], returned.at[my_rows(me)], s_ret, r_ret, seq=to
                ).start()

    def step(t, carry):
        pl.when(t < NG)(lambda: gather(t))
        pl.when((t >= 1) & (t < NG + 1))(lambda: forward(t - 1))
        pl.when((t >= 2) & (t < NG + 2))(lambda: serve(t - 2))
        pl.when((t >= 3) & (t < NG + 3))(lambda: reduce_pair(t - 3))
        pl.when(t >= 4)(lambda: reduce_plane(t - 4))
        return carry

    lax.fori_loop(0, NG + 4, step, 0)
    returned[my_rows(me), :] = summed[my_rows(me), :]

    lane = lax.broadcasted_iota(jnp.int32, (TOK, NSEQ * CAP), 1).astype(F32)
    picks = [(lane == columns(places[j])[:, 0:1]).astype(BF16) for j in range(2)]
    mixes = [columns(mix_ref[j : j + 1, :])[:, 0:1] for j in range(2)]
    others = (NSEQ - 1) * CAP
    remote(
        returned.at[0:others], returned.at[0:others], s_ret, r_ret, seq=me
    ).wait_recv()
    for c in range(PART // HD):
        lanes = slice(c * HD, (c + 1) * HD)
        out_ref[:, lanes] = (
            mid_ref[:, lanes].astype(F32)
            + (
                nn(picks[0], returned[:, lanes]) * mixes[0]
                + nn(picks[1], returned[:, lanes]) * mixes[1]
            )
        ).astype(BF16)

    remote(
        outgoing.at[0 : NSEQ - 1], outgoing.at[0 : NSEQ - 1], s_disp, r_disp.at[0], seq=me
    ).wait_send()
    remote(
        rows_in.at[0 : NX - 1], rows_in.at[0 : NX - 1], s_gath, r_gath.at[0, 0], head=hd
    ).wait_send()
    remote(rows_in.at[0:NX], rows_in.at[0:NX], s_fwd, r_fwd.at[0], head=hd).wait_send()
    remote(pair_in, pair_in, s_pair, r_pair.at[0], head=hd).wait_send()
    remote(
        plane_in.at[0 : NX - 1], plane_in.at[0 : NX - 1], s_plane, r_plane.at[0], head=hd
    ).wait_send()
    remote(
        returned.at[0:others], returned.at[0:others], s_ret, r_ret, seq=me
    ).wait_send()


def experts(middle, rout_t, mix_t, norm_gain, gate_t, up_t, down):
    vmem = pl.BlockSpec(memory_space=pltpu.VMEM)
    anywhere = pl.BlockSpec(memory_space=pl.ANY)
    dma = pltpu.SemaphoreType.DMA
    slots = NSEQ * CAP
    return pl.pallas_call(
        expert_kernel,
        out_shape=jax.ShapeDtypeStruct((TOK, PART), BF16),
        in_specs=[vmem] * 4 + [anywhere] * 3,
        out_specs=vmem,
        scratch_shapes=[
            pltpu.VMEM((FF, D), BF16),
            pltpu.VMEM((FF, D), BF16),
            pltpu.VMEM((FF, D), BF16),
            pltpu.VMEM((NSEQ, CAP, PART), BF16),
            pltpu.VMEM((NHEAD, slots, PART), BF16),
            pltpu.VMEM((GROWS, D), BF16),
            pltpu.VMEM((2, NX, slots, PART), BF16),
            pltpu.VMEM((NX, slots, PART), BF16),
            pltpu.VMEM((NX, slots, PART), BF16),
            pltpu.VMEM((NX, slots, PART), BF16),
            pltpu.VMEM((slots, PART), BF16),
            pltpu.VMEM((slots, PART), BF16),
            dma((3,)),
            dma,
            dma((NG,)),
            dma,
            dma((NG, NX)),
            dma,
            dma((NG,)),
            dma,
            dma((NG,)),
            dma,
            dma((NG,)),
            dma,
            dma,
        ],
        compiler_params=pltpu.CompilerParams(
            collective_id=1, has_side_effects=True, vmem_limit_bytes=VMEM_LIMIT
        ),
        name="experts",
    )(middle, rout_t, mix_t, norm_gain, gate_t, up_t, down)


def shards(
    queries,
    key_vectors,
    value_vectors,
    log_decay,
    doc_ids,
    head_gain,
    output_weight,
    residual,
    norm_gain,
    routing,
    route_weights,
    gate_weight,
    up_weight,
    down_weight,
):
    middle = attention(
        queries,
        key_vectors,
        value_vectors,
        log_decay.T,
        doc_ids.reshape(1, -1),
        head_gain.reshape(1, -1),
        output_weight.T,
        residual,
    )
    return experts(
        middle,
        routing.T,
        route_weights.T,
        norm_gain.reshape(1, -1),
        gate_weight[0].T,
        up_weight[0].T,
        down_weight[0],
    )


def solution(mesh):
    in_specs = (
        P("seq", "head"),
        P("seq", "head"),
        P("seq", "head"),
        P("seq", "head"),
        P("seq"),
        P("head"),
        P("head", "seq"),
        P("seq", "head"),
        P(),
        P("seq", None),
        P("seq", None),
        P("seq", None, "head"),
        P("seq", None, "head"),
        P("seq", "head", None),
    )
    return jax.shard_map(
        shards, mesh=mesh, in_specs=in_specs, out_specs=P("seq", "head"), check_vma=False
    )
```

```python
import functools

import jax
import jax.numpy as jnp
from jax import lax
from jax.experimental import pallas as pl
from jax.experimental.pallas import tpu as pltpu
from jax.sharding import PartitionSpec as P

MESH = pl.DeviceIdType.MESH
F32, BF16 = jnp.float32, jnp.bfloat16
EPSILON = 1e-06
NZ, NY, NX = 8, 4, 4
NSEQ, NHEAD = NZ * NY, 2 * NX
TOK, HEADS, HD = 128, 8, 128
WCOLS = 96
PART = 384
D = PART * NHEAD
CAP = 16
NG = 4
GSRC = NSEQ // NG
GROWS = GSRC * CAP
FF = 576
VMEM_LIMIT = 60 * 1024 * 1024


def nt(a, b):
    return lax.dot_general(a, b, (((1,), (1,)), ((), ())), preferred_element_type=F32)


def nn(a, b):
    return jnp.dot(a, b, preferred_element_type=F32)


def remote(src, dst, send_sem, recv_sem, **device):
    return pltpu.make_async_remote_copy(
        src_ref=src,
        dst_ref=dst,
        send_sem=send_sem,
        recv_sem=recv_sem,
        device_id=device,
        device_id_type=MESH,
    )


def greet(me, hd):
    barrier = pltpu.get_barrier_semaphore()

    @pl.loop(1, NSEQ)
    def _(d):
        pl.semaphore_signal(
            barrier, inc=1, device_id={"seq": lax.rem(me + d, NSEQ)}, device_id_type=MESH
        )

    @pl.loop(1, NHEAD)
    def _(d):
        pl.semaphore_signal(
            barrier, inc=1, device_id={"head": lax.rem(hd + d, NHEAD)}, device_id_type=MESH
        )

    return barrier


def columns(row):
    return jnp.transpose(jnp.broadcast_to(row, (TOK, TOK)))


def attention_kernel(
    q_ref,
    k_ref,
    v_ref,
    ld_ref,
    doc_ref,
    hg_ref,
    w_ref,
    res_ref,
    mid_ref,
    decay,
    own_state,
    own_info,
    all_state,
    all_info,
    own_carry,
    all_carry,
    inner,
    attended,
    weight,
    partial,
    paired,
    summed,
    arrived,
    column_out,
    column_in,
    s_state,
    r_state,
    s_info,
    r_info,
    s_carry,
    r_carry,
    s_att,
    r_att,
    s_w,
    r_w,
    s_pair,
    r_pair,
    s_part,
    r_part,
    s_col,
    r_col,
):
    me, hd = lax.axis_index("seq"), lax.axis_index("head")
    zi, yi = me // NY, lax.rem(me, NY)
    xi, core = hd // 2, lax.rem(hd, 2)
    partner = xi * 2 + 1 - core
    barrier = greet(me, hd)

    rows = lax.broadcasted_iota(jnp.int32, (TOK, TOK), 0)
    cols = lax.broadcasted_iota(jnp.int32, (TOK, TOK), 1)
    upper = (rows <= cols).astype(F32)
    sums = jnp.dot(
        ld_ref[...], upper, preferred_element_type=F32, precision=lax.Precision.HIGHEST
    )
    decay[...] = sums
    last = sums[:, TOK - 1 : TOK]
    doc = doc_ref[...].astype(F32)
    doc_first, doc_last = doc[:, 0:1], doc[:, TOK - 1 : TOK]
    tail = jnp.exp(last - sums) * (doc == doc_last).astype(F32)
    gain = jnp.exp(last) * (doc_first == doc_last).astype(F32)
    lane = lax.broadcasted_iota(jnp.int32, (HEADS, TOK), 1)
    info = jnp.where(lane < 32, gain, jnp.where(lane < 64, doc_first, doc_last))
    for h in range(HEADS):
        own_info[h] = info[h : h + 1, :]
    for h in range(HEADS):
        lanes = slice(h * HD, (h + 1) * HD)
        key_t = jnp.transpose(k_ref[:, lanes].astype(F32))
        state = nn((key_t * tail[h : h + 1, :]).astype(BF16), v_ref[:, lanes])
        own_state[4 * h : 4 * h + 4] = state.astype(BF16).reshape(4, 32, HD)

    pl.semaphore_wait(barrier, NSEQ + NHEAD - 2)

    @pl.loop(1, NSEQ)
    def _(d):
        to = lax.rem(me + d, NSEQ)
        remote(own_info.at[to // 4], all_info.at[me], s_info, r_info, seq=to).start()
        remote(own_state.at[to], all_state.at[me], s_state, r_state, seq=to).start()

    all_state[me] = own_state[me]
    all_info[me] = own_info[me // 4]

    def w_rows(z, start=0, size=WCOLS):
        return pl.ds(pl.multiple_of(lax.rem(z + NZ, NZ) * WCOLS + start, 16), size)

    right = lax.rem(zi + 1, NZ) * NY + yi
    left = lax.rem(zi + NZ - 1, NZ) * NY + yi
    half = WCOLS // 2

    def w_copy(rows, k, to, side):
        block = weight.at[rows]
        return remote(block, block, s_w, r_w.at[side, k], seq=to)

    def w_step(k):
        w_copy(w_rows(zi - 1 - k), k, me, 0).wait_recv()
        from_left = w_rows(zi - 1 - k) if k < 2 else w_rows(zi - 1 - k, 0, half)
        w_copy(from_left, k + 1, right, 0).start()
        w_copy(w_rows(zi + 1 + k), k, me, 1).wait_recv()
        from_right = w_rows(zi + 1 + k) if k < 2 else w_rows(zi + 1 + k, half, half)
        w_copy(from_right, k + 1, left, 1).start()

    remote(w_ref, weight.at[w_rows(zi)], s_w, r_w.at[0, 0], seq=right).start()
    remote(w_ref, weight.at[w_rows(zi)], s_w, r_w.at[1, 0], seq=left).start()

    doc_rows = jnp.broadcast_to(doc, (TOK, TOK))
    kept = (cols <= rows) & (jnp.transpose(doc_rows) == doc_rows)
    for h in range(HEADS):
        lanes = slice(h * HD, (h + 1) * HD)
        decay_row = jnp.broadcast_to(decay[h : h + 1, :], (TOK, TOK))
        gap = jnp.transpose(decay_row) - decay_row
        factor = jnp.where(kept, jnp.exp(jnp.minimum(gap, 0.0)), 0.0)
        weighted = (nt(q_ref[:, lanes], k_ref[:, lanes]) * factor).astype(BF16)
        inner[:, lanes] = nn(weighted, v_ref[:, lanes])
    weight[w_rows(zi), :] = w_ref[...]

    others = NSEQ - 1
    remote(
        own_state.at[0:others], all_state.at[0:others], s_state, r_state, seq=me
    ).wait_recv()
    remote(
        all_info.at[0:others], all_info.at[0:others], s_info, r_info, seq=me
    ).wait_recv()

    def scan(b, carry):
        carried, before = carry
        own_carry[b] = carried.astype(BF16)
        row = all_info[b]
        through = jnp.where(row[:, 32:33] == before, row[:, 0:1], 0.0)
        return all_state[b].astype(F32) + through * carried, row[:, 64:65]

    lax.fori_loop(
        0,
        NSEQ,
        scan,
        (jnp.zeros((32, HD), F32), jnp.full((1, 1), -1.0, F32)),
        unroll=4,
    )

    @pl.loop(1, NSEQ)
    def _(d):
        to = lax.rem(me + d, NSEQ)
        remote(own_carry.at[to], all_carry.at[me], s_carry, r_carry, seq=to).start()

    all_carry[me] = own_carry[me]
    before_doc = all_info[jnp.maximum(me - 1, 0)][:, 64:65]
    before_doc = jnp.where(jnp.full((1, 1), me, jnp.int32) == 0, -1.0, before_doc)
    w_step(0)
    reach = jnp.exp(decay[...]) * (doc == before_doc).astype(F32)
    remote(
        own_carry.at[0:others], all_carry.at[0:others], s_carry, r_carry, seq=me
    ).wait_recv()
    w_step(1)
    for h in range(HEADS):
        lanes = slice(h * HD, (h + 1) * HD)
        carried = all_carry[4 * h : 4 * h + 4].reshape(HD, HD)
        raw = inner[:, lanes] + nn(q_ref[:, lanes], carried) * columns(reach[h : h + 1, :])
        scale = lax.rsqrt(jnp.mean(raw * raw, axis=1, keepdims=True) + EPSILON)
        attended[yi, :, lanes] = (raw * scale * hg_ref[:, lanes]).astype(BF16)
        if h % 2 == 1:
            pair = slice((h - 1) * HD, (h + 1) * HD)
            for d in range(1, NY):
                to = zi * NY + lax.rem(yi + d, NY)
                remote(
                    attended.at[yi, :, pair],
                    attended.at[yi, :, pair],
                    s_att,
                    r_att.at[yi],
                    seq=to,
                ).start()

    w_step(2)
    w_copy(w_rows(zi + 4, 0, half), 3, me, 0).wait_recv()
    w_copy(w_rows(zi + 4, half, half), 3, me, 1).wait_recv()

    def project(i):
        y = lax.rem(yi + NY - i, NY)

        @pl.when(i > 0)
        def _():
            remote(attended.at[y], attended.at[y], s_att, r_att.at[y], seq=me).wait_recv()

        partial[y] = nt(weight[...], attended[y]).astype(BF16).reshape(NX, 2, WCOLS, TOK)
        remote(
            partial.at[y, :, 1 - core], paired.at[y], s_pair, r_pair.at[y], head=partner
        ).start()

    def pair_sum(i):
        y = lax.rem(yi + NY - i, NY)
        remote(paired.at[y], paired.at[y], s_pair, r_pair.at[y], head=hd).wait_recv()
        for d in (2, 1, 3, 0):
            x = lax.rem(xi + d, NX)
            both = (
                partial[y, x, core].astype(F32) + paired[y, x].astype(F32)
            ).astype(BF16)
            if d:
                summed[y, x] = both
                remote(
                    summed.at[y, x],
                    arrived.at[y, xi],
                    s_part,
                    r_part.at[y],
                    head=x * 2 + core,
                ).start()
            else:
                arrived[y, xi] = both

    def plane_sum(i):
        y = lax.rem(yi + NY - i, NY)
        remote(
            arrived.at[y, 0 : NX - 1],
            arrived.at[y, 0 : NX - 1],
            s_part,
            r_part.at[y],
            head=hd,
        ).wait_recv()
        total = arrived[y, 0].astype(F32)
        for x in range(1, NX):
            total = total + arrived[y, x].astype(F32)
        column_out[y] = total.astype(BF16)

        @pl.when(i > 0)
        def _():
            remote(
                column_out.at[y], column_in.at[yi], s_col, r_col, seq=zi * NY + y
            ).start()

        @pl.when(i == 0)
        def _():
            column_in[yi] = total.astype(BF16)

    def step(t, carry):
        pl.when(t < NY)(lambda: project(t))
        pl.when((t >= 1) & (t < NY + 1))(lambda: pair_sum(t - 1))
        pl.when(t >= 2)(lambda: plane_sum(t - 2))
        return carry

    lax.fori_loop(0, NY + 2, step, 0)
    remote(
        column_in.at[0 : NY - 1], column_in.at[0 : NY - 1], s_col, r_col, seq=me
    ).wait_recv()
    for c in range(PART // HD):
        lanes = slice(c * HD, (c + 1) * HD)
        slab = column_in[...].astype(F32).reshape(PART, TOK)[c * HD : (c + 1) * HD, :]
        mid_ref[:, lanes] = (res_ref[:, lanes].astype(F32) + jnp.transpose(slab)).astype(BF16)

    remote(
        own_state.at[0:others], all_state.at[0:others], s_state, r_state, seq=me
    ).wait_send()
    remote(
        all_info.at[0:others], all_info.at[0:others], s_info, r_info, seq=me
    ).wait_send()
    remote(
        own_carry.at[0:others], all_carry.at[0:others], s_carry, r_carry, seq=me
    ).wait_send()
    remote(attended.at[0:3], attended.at[0:3], s_att, r_att.at[0], seq=me).wait_send()
    w_copy(pl.ds(0, (NZ - 1) * WCOLS), 0, me, 0).wait_send()
    remote(paired, paired, s_pair, r_pair.at[0], head=hd).wait_send()
    remote(
        arrived.at[:, 0 : NX - 1],
        arrived.at[:, 0 : NX - 1],
        s_part,
        r_part.at[0],
        head=hd,
    ).wait_send()
    remote(
        column_in.at[0 : NY - 1], column_in.at[0 : NY - 1], s_col, r_col, seq=me
    ).wait_send()


def attention(q, k, v, ld_t, doc, gain, w_t, residual):
    vmem = pl.BlockSpec(memory_space=pltpu.VMEM)
    dma = pltpu.SemaphoreType.DMA
    return pl.pallas_call(
        attention_kernel,
        out_shape=jax.ShapeDtypeStruct((TOK, PART), BF16),
        in_specs=[vmem] * 8,
        out_specs=vmem,
        scratch_shapes=[
            pltpu.VMEM((HEADS, TOK), F32),
            pltpu.VMEM((NSEQ, 32, HD), BF16),
            pltpu.VMEM((HEADS, 1, TOK), F32),
            pltpu.VMEM((NSEQ, 32, HD), BF16),
            pltpu.VMEM((NSEQ, 1, TOK), F32),
            pltpu.VMEM((NSEQ, 32, HD), BF16),
            pltpu.VMEM((NSEQ, 32, HD), BF16),
            pltpu.VMEM((TOK, HEADS * HD), F32),
            pltpu.VMEM((NY, TOK, HEADS * HD), BF16),
            pltpu.VMEM((NZ * WCOLS, HEADS * HD), BF16),
            pltpu.VMEM((NY, NX, 2, WCOLS, TOK), BF16),
            pltpu.VMEM((NY, NX, WCOLS, TOK), BF16),
            pltpu.VMEM((NY, NX, WCOLS, TOK), BF16),
            pltpu.VMEM((NY, NX, WCOLS, TOK), BF16),
            pltpu.VMEM((NY, WCOLS, TOK), BF16),
            pltpu.VMEM((NY, WCOLS, TOK), BF16),
            dma,
            dma,
            dma,
            dma,
            dma,
            dma,
            dma,
            dma((NY,)),
            dma,
            dma((2, 4)),
            dma,
            dma((NY,)),
            dma,
            dma((NY,)),
            dma,
            dma,
        ],
        compiler_params=pltpu.CompilerParams(
            collective_id=0, has_side_effects=True, vmem_limit_bytes=VMEM_LIMIT
        ),
        name="attention",
    )(q, k, v, ld_t, doc, gain, w_t, residual)


def expert_kernel(
    mid_ref,
    rout_ref,
    mix_ref,
    ng_ref,
    gate_hbm,
    up_hbm,
    down_hbm,
    out_ref,
    gate,
    up,
    down,
    outgoing,
    rows_in,
    normed,
    result,
    pair_in,
    pair_sum,
    plane_in,
    summed,
    returned,
    s_load,
    s_disp,
    r_disp,
    s_gath,
    r_gath,
    s_fwd,
    r_fwd,
    s_pair,
    r_pair,
    s_plane,
    r_plane,
    s_ret,
    r_ret,
):
    me, hd = lax.axis_index("seq"), lax.axis_index("head")
    xi, core = hd // 2, lax.rem(hd, 2)
    partner = xi * 2 + 1 - core
    group = me // GSRC
    barrier = greet(me, hd)
    loads = [
        pltpu.make_async_copy(gate_hbm, gate, s_load.at[0]),
        pltpu.make_async_copy(up_hbm, up, s_load.at[1]),
        pltpu.make_async_copy(down_hbm, down, s_load.at[2]),
    ]
    for load in loads:
        load.start()

    expert = lax.broadcasted_iota(jnp.int32, (NSEQ, TOK), 0)
    hits = [(expert == rout_ref[j : j + 1, :]).astype(F32) for j in range(2)]
    earlier = (
        lax.broadcasted_iota(jnp.int32, (TOK, TOK), 0)
        < lax.broadcasted_iota(jnp.int32, (TOK, TOK), 1)
    ).astype(BF16)
    count = nn((hits[0] + hits[1]).astype(BF16), earlier)
    places = [
        rout_ref[j : j + 1, :].astype(F32) * CAP
        + jnp.sum(hits[j] * count, axis=0, keepdims=True)
        for j in range(2)
    ]
    slot = lax.broadcasted_iota(jnp.int32, (NSEQ * CAP, TOK), 0).astype(F32)
    chosen = (slot == places[0]).astype(F32) + (slot == places[1]).astype(F32)
    outgoing[...] = (
        nn(chosen.astype(BF16), mid_ref[...]).astype(BF16).reshape(NSEQ, CAP, PART)
    )

    pl.semaphore_wait(barrier, NSEQ + NHEAD - 2)

    def my_rows(index):
        return pl.ds(pl.multiple_of(index * CAP, CAP), CAP)

    def group_rows(index):
        return pl.ds(pl.multiple_of(index * GROWS, GROWS), GROWS)

    @pl.loop(1, NSEQ)
    def _(d):
        to = lax.rem(me + d, NSEQ)
        remote(
            outgoing.at[to],
            rows_in.at[hd, my_rows(me)],
            s_disp,
            r_disp.at[group],
            seq=to,
        ).start()

    rows_in[hd, my_rows(me), :] = outgoing[me]

    def gather(i):
        g = lax.rem(group + NG - i, NG)
        part = group_rows(g)

        @pl.when(i == 0)
        def _():
            remote(
                outgoing.at[0 : GSRC - 1],
                outgoing.at[0 : GSRC - 1],
                s_disp,
                r_disp.at[g],
                seq=me,
            ).wait_recv()

        @pl.when(i > 0)
        def _():
            remote(
                outgoing.at[0:GSRC], outgoing.at[0:GSRC], s_disp, r_disp.at[g], seq=me
            ).wait_recv()

        for d in (2, 1, 3):
            to = lax.rem(xi + d, NX) * 2 + core
            remote(
                rows_in.at[hd, part],
                rows_in.at[hd, part],
                s_gath,
                r_gath.at[g, xi],
                head=to,
            ).start()
        remote(
            rows_in.at[hd, part], rows_in.at[hd, part], s_fwd, r_fwd.at[g], head=partner
        ).start()

    def forward(i):
        g = lax.rem(group + NG - i, NG)
        part = group_rows(g)
        for d in (1, 3, 2):
            x = lax.rem(xi + d, NX)
            block = rows_in.at[x * 2 + core, part]
            remote(block, block, s_gath, r_gath.at[g, x], head=hd).wait_recv()
            remote(block, block, s_fwd, r_fwd.at[g], head=partner).start()

    def serve(i):
        g = lax.rem(group + NG - i, NG)
        part = group_rows(g)

        @pl.when(i == 0)
        def _():
            for load in loads:
                load.wait()

        remote(
            rows_in.at[0:NX, 0:GROWS], rows_in.at[0:NX, 0:GROWS], s_fwd, r_fwd.at[g], head=hd
        ).wait_recv()
        squares = jnp.zeros((GROWS, HD), F32)
        for h in range(NHEAD):
            block = rows_in[h, part, :].astype(F32)
            block = block * block
            for c in range(PART // HD):
                squares = squares + block[:, c * HD : (c + 1) * HD]
        scale = lax.rsqrt(jnp.sum(squares, axis=1, keepdims=True) / D + EPSILON)
        for h in range(NHEAD):
            lanes = slice(h * PART, (h + 1) * PART)
            normed[:, lanes] = (
                rows_in[h, part, :].astype(F32) * scale * ng_ref[:, lanes]
            ).astype(BF16)
        gated = nt(normed[...], gate[...])
        upped = nt(normed[...], up[...])
        hidden = (gated / (1.0 + jnp.exp(-gated)) * upped).astype(BF16)
        for h in range(NHEAD):
            lanes = slice(h * PART, (h + 1) * PART)
            result[h % 2, h // 2, part, :] = nn(hidden, down[:, lanes]).astype(BF16)
        remote(
            result.at[1 - core, :, part],
            pair_in.at[:, part],
            s_pair,
            r_pair.at[g],
            head=partner,
        ).start()

    def reduce_pair(i):
        g = lax.rem(group + NG - i, NG)
        part = group_rows(g)
        remote(
            pair_in.at[:, part], pair_in.at[:, part], s_pair, r_pair.at[g], head=hd
        ).wait_recv()
        for d in (2, 1, 3, 0):
            x = lax.rem(xi + d, NX)
            pair_sum[x, part, :] = (
                result[core, x, part, :].astype(F32) + pair_in[x, part, :].astype(F32)
            ).astype(BF16)
            if d:
                remote(
                    pair_sum.at[x, part],
                    plane_in.at[xi, part],
                    s_plane,
                    r_plane.at[g],
                    head=x * 2 + core,
                ).start()

    def reduce_plane(i):
        g = lax.rem(group + NG - i, NG)
        part = group_rows(g)
        remote(
            plane_in.at[0 : NX - 1, part],
            plane_in.at[0 : NX - 1, part],
            s_plane,
            r_plane.at[g],
            head=hd,
        ).wait_recv()
        total = pair_sum[xi, part, :].astype(F32)
        for d in range(1, NX):
            total = total + plane_in[lax.rem(xi + d, NX), part, :].astype(F32)
        summed[part, :] = total.astype(BF16)

        @pl.loop(0, GSRC)
        def _(j):
            to = g * GSRC + j

            @pl.when(to != me)
            def _():
                remote(
                    summed.at[my_rows(to)], returned.at[my_rows(me)], s_ret, r_ret, seq=to
                ).start()

    def step(t, carry):
        pl.when(t < NG)(lambda: gather(t))
        pl.when((t >= 1) & (t < NG + 1))(lambda: forward(t - 1))
        pl.when((t >= 2) & (t < NG + 2))(lambda: serve(t - 2))
        pl.when((t >= 3) & (t < NG + 3))(lambda: reduce_pair(t - 3))
        pl.when(t >= 4)(lambda: reduce_plane(t - 4))
        return carry

    lax.fori_loop(0, NG + 4, step, 0)
    returned[my_rows(me), :] = summed[my_rows(me), :]

    lane = lax.broadcasted_iota(jnp.int32, (TOK, NSEQ * CAP), 1).astype(F32)
    picks = [(lane == columns(places[j])[:, 0:1]).astype(BF16) for j in range(2)]
    mixes = [columns(mix_ref[j : j + 1, :])[:, 0:1] for j in range(2)]
    others = (NSEQ - 1) * CAP
    remote(
        returned.at[0:others], returned.at[0:others], s_ret, r_ret, seq=me
    ).wait_recv()
    for c in range(PART // HD):
        lanes = slice(c * HD, (c + 1) * HD)
        out_ref[:, lanes] = (
            mid_ref[:, lanes].astype(F32)
            + (
                nn(picks[0], returned[:, lanes]) * mixes[0]
                + nn(picks[1], returned[:, lanes]) * mixes[1]
            )
        ).astype(BF16)

    remote(
        outgoing.at[0 : NSEQ - 1], outgoing.at[0 : NSEQ - 1], s_disp, r_disp.at[0], seq=me
    ).wait_send()
    remote(
        rows_in.at[0 : NX - 1], rows_in.at[0 : NX - 1], s_gath, r_gath.at[0, 0], head=hd
    ).wait_send()
    remote(rows_in.at[0:NX], rows_in.at[0:NX], s_fwd, r_fwd.at[0], head=hd).wait_send()
    remote(pair_in, pair_in, s_pair, r_pair.at[0], head=hd).wait_send()
    remote(
        plane_in.at[0 : NX - 1], plane_in.at[0 : NX - 1], s_plane, r_plane.at[0], head=hd
    ).wait_send()
    remote(
        returned.at[0:others], returned.at[0:others], s_ret, r_ret, seq=me
    ).wait_send()


def experts(middle, rout_t, mix_t, norm_gain, gate_t, up_t, down):
    vmem = pl.BlockSpec(memory_space=pltpu.VMEM)
    anywhere = pl.BlockSpec(memory_space=pl.ANY)
    dma = pltpu.SemaphoreType.DMA
    slots = NSEQ * CAP
    return pl.pallas_call(
        expert_kernel,
        out_shape=jax.ShapeDtypeStruct((TOK, PART), BF16),
        in_specs=[vmem] * 4 + [anywhere] * 3,
        out_specs=vmem,
        scratch_shapes=[
            pltpu.VMEM((FF, D), BF16),
            pltpu.VMEM((FF, D), BF16),
            pltpu.VMEM((FF, D), BF16),
            pltpu.VMEM((NSEQ, CAP, PART), BF16),
            pltpu.VMEM((NHEAD, slots, PART), BF16),
            pltpu.VMEM((GROWS, D), BF16),
            pltpu.VMEM((2, NX, slots, PART), BF16),
            pltpu.VMEM((NX, slots, PART), BF16),
            pltpu.VMEM((NX, slots, PART), BF16),
            pltpu.VMEM((NX, slots, PART), BF16),
            pltpu.VMEM((slots, PART), BF16),
            pltpu.VMEM((slots, PART), BF16),
            dma((3,)),
            dma,
            dma((NG,)),
            dma,
            dma((NG, NX)),
            dma,
            dma((NG,)),
            dma,
            dma((NG,)),
            dma,
            dma((NG,)),
            dma,
            dma,
        ],
        compiler_params=pltpu.CompilerParams(
            collective_id=1, has_side_effects=True, vmem_limit_bytes=VMEM_LIMIT
        ),
        name="experts",
    )(middle, rout_t, mix_t, norm_gain, gate_t, up_t, down)


def shards(
    queries,
    key_vectors,
    value_vectors,
    log_decay,
    doc_ids,
    head_gain,
    output_weight,
    residual,
    norm_gain,
    routing,
    route_weights,
    gate_weight,
    up_weight,
    down_weight,
):
    middle = attention(
        queries,
        key_vectors,
        value_vectors,
        log_decay.T,
        doc_ids.reshape(1, -1),
        head_gain.reshape(1, -1),
        output_weight.T,
        residual,
    )
    return experts(
        middle,
        routing.T,
        route_weights.T,
        norm_gain.reshape(1, -1),
        gate_weight[0].T,
        up_weight[0].T,
        down_weight[0],
    )


def solution(mesh):
    in_specs = (
        P("seq", "head"),
        P("seq", "head"),
        P("seq", "head"),
        P("seq", "head"),
        P("seq"),
        P("head"),
        P("head", "seq"),
        P("seq", "head"),
        P(),
        P("seq", None),
        P("seq", None),
        P("seq", None, "head"),
        P("seq", None, "head"),
        P("seq", "head", None),
    )
    return jax.shard_map(
        shards, mesh=mesh, in_specs=in_specs, out_specs=P("seq", "head"), check_vma=False
    )
```

```python
import functools

import jax
import jax.numpy as jnp
from jax import lax
from jax.experimental import pallas as pl
from jax.experimental.pallas import tpu as pltpu
from jax.sharding import PartitionSpec as P

MESH = pl.DeviceIdType.MESH
F32, BF16 = jnp.float32, jnp.bfloat16
EPSILON = 1e-06
NZ, NY, NX = 8, 4, 4
NSEQ, NHEAD = NZ * NY, 2 * NX
TOK, HEADS, HD = 128, 8, 128
WCOLS = 96
PART = 384
D = PART * NHEAD
CAP = 16
NG = 4
GSRC = NSEQ // NG
GROWS = GSRC * CAP
SLOTS = NSEQ * CAP
FF = 576
VMEM_LIMIT = 60 * 1024 * 1024


def nt(a, b):
    return lax.dot_general(a, b, (((1,), (1,)), ((), ())), preferred_element_type=F32)


def nn(a, b):
    return jnp.dot(a, b, preferred_element_type=F32)


def remote(src, dst, send_sem, recv_sem, **device):
    return pltpu.make_async_remote_copy(
        src_ref=src,
        dst_ref=dst,
        send_sem=send_sem,
        recv_sem=recv_sem,
        device_id=device,
        device_id_type=MESH,
    )


def greet(me, hd):
    barrier = pltpu.get_barrier_semaphore()

    @pl.loop(1, NSEQ)
    def _(d):
        pl.semaphore_signal(
            barrier, inc=1, device_id={"seq": lax.rem(me + d, NSEQ)}, device_id_type=MESH
        )

    @pl.loop(1, NHEAD)
    def _(d):
        pl.semaphore_signal(
            barrier, inc=1, device_id={"head": lax.rem(hd + d, NHEAD)}, device_id_type=MESH
        )

    return barrier


def turn(i):
    return i + i // 2 - 2 * (i // 3)


def columns(row):
    return jnp.transpose(jnp.broadcast_to(row, (TOK, TOK)))


def layer_kernel(
    q_ref,
    k_ref,
    v_ref,
    ld_ref,
    doc_ref,
    hg_ref,
    w_ref,
    res_ref,
    rout_ref,
    mix_ref,
    ng_ref,
    gate_hbm,
    up_hbm,
    down_hbm,
    out_ref,
    decay,
    own_state,
    own_info,
    all_state,
    all_info,
    own_carry,
    all_carry,
    inner,
    attended,
    weight,
    partial,
    paired,
    half_sum,
    arrived,
    column_out,
    column_in,
    middle,
    chosen_rows,
    picks,
    mixes,
    gate,
    up,
    down,
    outgoing,
    rows_in,
    normed,
    result,
    pair_in,
    far_sum,
    ring_in,
    near_sum,
    plane_in,
    summed,
    returned,
    s_state,
    r_state,
    s_info,
    r_info,
    s_carry,
    r_carry,
    s_att,
    r_att,
    s_w,
    r_w,
    s_pp,
    r_pp,
    s_part,
    r_part,
    s_col,
    r_col,
    s_load,
    s_disp,
    r_disp,
    s_gath,
    r_gath,
    s_fwd,
    r_fwd,
    s_pair,
    r_pair,
    s_ring,
    r_ring,
    s_plane,
    r_plane,
    s_ret,
    r_ret,
):
    me, hd = lax.axis_index("seq"), lax.axis_index("head")
    zi, yi = me // NY, lax.rem(me, NY)
    xi, core = hd // 2, lax.rem(hd, 2)
    partner = xi * 2 + 1 - core
    group = me // GSRC
    barrier = greet(me, hd)
    loads = [
        pltpu.make_async_copy(gate_hbm, gate, s_load.at[0]),
        pltpu.make_async_copy(up_hbm, up, s_load.at[1]),
        pltpu.make_async_copy(down_hbm, down, s_load.at[2]),
    ]
    for load in loads:
        load.start()

    rows = lax.broadcasted_iota(jnp.int32, (TOK, TOK), 0)
    cols = lax.broadcasted_iota(jnp.int32, (TOK, TOK), 1)
    upper = (rows <= cols).astype(F32)
    sums = jnp.dot(
        ld_ref[...], upper, preferred_element_type=F32, precision=lax.Precision.HIGHEST
    )
    decay[...] = sums
    last = sums[:, TOK - 1 : TOK]
    doc = doc_ref[...].astype(F32)
    doc_first, doc_last = doc[:, 0:1], doc[:, TOK - 1 : TOK]
    tail = jnp.exp(last - sums) * (doc == doc_last).astype(F32)
    gain = jnp.exp(last) * (doc_first == doc_last).astype(F32)
    lane = lax.broadcasted_iota(jnp.int32, (HEADS, TOK), 1)
    info = jnp.where(lane < 32, gain, jnp.where(lane < 64, doc_first, doc_last))
    for h in range(HEADS):
        own_info[h] = info[h : h + 1, :]
    for h in range(HEADS):
        lanes = slice(h * HD, (h + 1) * HD)
        key_t = jnp.transpose(k_ref[:, lanes].astype(F32))
        state = nn((key_t * tail[h : h + 1, :]).astype(BF16), v_ref[:, lanes])
        own_state[4 * h : 4 * h + 4] = state.astype(BF16).reshape(4, 32, HD)

    pl.semaphore_wait(barrier, NSEQ + NHEAD - 2)

    @pl.loop(1, NSEQ)
    def _(d):
        to = lax.rem(me + d, NSEQ)
        remote(own_info.at[to // 4], all_info.at[me], s_info, r_info, seq=to).start()
        remote(own_state.at[to], all_state.at[me], s_state, r_state, seq=to).start()

    all_state[me] = own_state[me]
    all_info[me] = own_info[me // 4]

    def w_rows(z, start=0, size=WCOLS):
        return pl.ds(pl.multiple_of(lax.rem(z + NZ, NZ) * WCOLS + start, 16), size)

    right = lax.rem(zi + 1, NZ) * NY + yi
    left = lax.rem(zi + NZ - 1, NZ) * NY + yi
    half = WCOLS // 2

    def w_copy(rows, k, to, side):
        block = weight.at[rows]
        return remote(block, block, s_w, r_w.at[side, k], seq=to)

    def w_step(k):
        w_copy(w_rows(zi - 1 - k), k, me, 0).wait_recv()
        from_left = w_rows(zi - 1 - k) if k < 2 else w_rows(zi - 1 - k, 0, half)
        w_copy(from_left, k + 1, right, 0).start()
        w_copy(w_rows(zi + 1 + k), k, me, 1).wait_recv()
        from_right = w_rows(zi + 1 + k) if k < 2 else w_rows(zi + 1 + k, half, half)
        w_copy(from_right, k + 1, left, 1).start()

    remote(w_ref, weight.at[w_rows(zi)], s_w, r_w.at[0, 0], seq=right).start()
    remote(w_ref, weight.at[w_rows(zi)], s_w, r_w.at[1, 0], seq=left).start()

    doc_rows = jnp.broadcast_to(doc, (TOK, TOK))
    kept = (cols <= rows) & (jnp.transpose(doc_rows) == doc_rows)
    for h in range(HEADS):
        lanes = slice(h * HD, (h + 1) * HD)
        decay_row = jnp.broadcast_to(decay[h : h + 1, :], (TOK, TOK))
        gap = jnp.transpose(decay_row) - decay_row
        factor = jnp.where(kept, jnp.exp(jnp.minimum(gap, 0.0)), 0.0)
        weighted = (nt(q_ref[:, lanes], k_ref[:, lanes]) * factor).astype(BF16)
        inner[:, lanes] = nn(weighted, v_ref[:, lanes])
    weight[w_rows(zi), :] = w_ref[...]
    expert = lax.broadcasted_iota(jnp.int32, (NSEQ, TOK), 0)
    hits = [(expert == rout_ref[j : j + 1, :]).astype(F32) for j in range(2)]
    earlier = (
        lax.broadcasted_iota(jnp.int32, (TOK, TOK), 0)
        < lax.broadcasted_iota(jnp.int32, (TOK, TOK), 1)
    ).astype(BF16)
    count = nn((hits[0] + hits[1]).astype(BF16), earlier)
    places = [
        rout_ref[j : j + 1, :].astype(F32) * CAP
        + jnp.sum(hits[j] * count, axis=0, keepdims=True)
        for j in range(2)
    ]
    slot = lax.broadcasted_iota(jnp.int32, (NSEQ * CAP, TOK), 0).astype(F32)
    chosen = (slot == places[0]).astype(F32) + (slot == places[1]).astype(F32)
    chosen_rows[...] = chosen.astype(BF16)
    lane = lax.broadcasted_iota(jnp.int32, (TOK, NSEQ * CAP), 1).astype(F32)
    for j in range(2):
        picks[j] = (lane == columns(places[j])[:, 0:1]).astype(BF16)
        mixes[j] = columns(mix_ref[j : j + 1, :])


    others = NSEQ - 1
    remote(
        own_state.at[0:others], all_state.at[0:others], s_state, r_state, seq=me
    ).wait_recv()
    remote(
        all_info.at[0:others], all_info.at[0:others], s_info, r_info, seq=me
    ).wait_recv()

    def scan(b, carry):
        carried, before = carry
        own_carry[b] = carried.astype(BF16)
        row = all_info[b]
        through = jnp.where(row[:, 32:33] == before, row[:, 0:1], 0.0)
        return all_state[b].astype(F32) + through * carried, row[:, 64:65]

    lax.fori_loop(
        0,
        NSEQ,
        scan,
        (jnp.zeros((32, HD), F32), jnp.full((1, 1), -1.0, F32)),
        unroll=4,
    )

    @pl.loop(1, NSEQ)
    def _(d):
        to = lax.rem(me + d, NSEQ)
        remote(own_carry.at[to], all_carry.at[me], s_carry, r_carry, seq=to).start()

    all_carry[me] = own_carry[me]
    before_doc = all_info[jnp.maximum(me - 1, 0)][:, 64:65]
    before_doc = jnp.where(jnp.full((1, 1), me, jnp.int32) == 0, -1.0, before_doc)
    w_step(0)
    reach = jnp.exp(decay[...]) * (doc == before_doc).astype(F32)
    remote(
        own_carry.at[0:others], all_carry.at[0:others], s_carry, r_carry, seq=me
    ).wait_recv()
    w_step(1)
    y_up = zi * NY + lax.rem(yi + 1, NY)
    y_down = zi * NY + lax.rem(yi + NY - 1, NY)

    def att_half(y, part):
        return attended.at[lax.rem(y + NY, NY), :, part * 512 : (part + 1) * 512]

    def att_wait(block, side, part):
        remote(block, block, s_att, r_att.at[side, part], seq=me).wait_recv()

    for h in range(HEADS):
        lanes = slice(h * HD, (h + 1) * HD)
        carried = all_carry[4 * h : 4 * h + 4].reshape(HD, HD)
        raw = inner[:, lanes] + nn(q_ref[:, lanes], carried) * columns(reach[h : h + 1, :])
        scale = lax.rsqrt(jnp.mean(raw * raw, axis=1, keepdims=True) + EPSILON)
        attended[yi, :, lanes] = (raw * scale * hg_ref[:, lanes]).astype(BF16)
        if h % 2 == 1:
            pair = slice((h - 1) * HD, (h + 1) * HD)
            block = attended.at[yi, :, pair]
            remote(block, block, s_att, r_att.at[0, h // 4], seq=y_up).start()
            remote(block, block, s_att, r_att.at[1, h // 4], seq=y_down).start()

    block = att_half(yi - 1, 0)
    att_wait(block, 0, 0)
    remote(block, block, s_att, r_att.at[2, 0], seq=y_up).start()
    w_step(2)
    block = att_half(yi + 1, 1)
    att_wait(block, 1, 1)
    remote(block, block, s_att, r_att.at[2, 1], seq=y_down).start()
    w_copy(w_rows(zi + 4, 0, half), 3, me, 0).wait_recv()
    w_copy(w_rows(zi + 4, half, half), 3, me, 1).wait_recv()

    def project(i):
        y = lax.rem(yi + NY - turn(i), NY)
        pl.when(i == 1)(lambda: att_wait(att_half(yi - 1, 1), 0, 1))
        pl.when(i == 2)(lambda: att_wait(att_half(yi + 1, 0), 1, 0))

        @pl.when(i == 3)
        def _():
            att_wait(att_half(yi + 2, 0), 2, 0)
            att_wait(att_half(yi + 2, 1), 2, 1)

        partial[y] = nt(weight[...], attended[y]).astype(BF16).reshape(NX, 2, WCOLS, TOK)
        remote(
            partial.at[y, :, 1 - core], paired.at[y], s_pp, r_pp.at[y], head=partner
        ).start()

    def pair_sum(i):
        y = lax.rem(yi + NY - turn(i), NY)
        remote(paired.at[y], paired.at[y], s_pp, r_pp.at[y], head=hd).wait_recv()
        for d in (2, 1, 3, 0):
            x = lax.rem(xi + d, NX)
            both = (
                partial[y, x, core].astype(F32) + paired[y, x].astype(F32)
            ).astype(BF16)
            if d:
                half_sum[y, x] = both
                remote(
                    half_sum.at[y, x],
                    arrived.at[y, xi],
                    s_part,
                    r_part.at[y],
                    head=x * 2 + core,
                ).start()
            else:
                arrived[y, xi] = both

    def plane_sum(i):
        y = lax.rem(yi + NY - turn(i), NY)
        remote(
            arrived.at[y, 0 : NX - 1],
            arrived.at[y, 0 : NX - 1],
            s_part,
            r_part.at[y],
            head=hd,
        ).wait_recv()
        total = arrived[y, 0].astype(F32)
        for x in range(1, NX):
            total = total + arrived[y, x].astype(F32)
        column_out[y] = total.astype(BF16)

        @pl.when(i > 0)
        def _():
            remote(
                column_out.at[y], column_in.at[yi], s_col, r_col, seq=zi * NY + y
            ).start()

        @pl.when(i == 0)
        def _():
            column_in[yi] = total.astype(BF16)

    def project_step(t, carry):
        pl.when(t < NY)(lambda: project(t))
        pl.when((t >= 1) & (t < NY + 1))(lambda: pair_sum(t - 1))
        pl.when(t >= 2)(lambda: plane_sum(t - 2))
        return carry

    lax.fori_loop(0, NY + 2, project_step, 0)
    remote(
        column_in.at[0 : NY - 1], column_in.at[0 : NY - 1], s_col, r_col, seq=me
    ).wait_recv()
    for c in range(PART // HD):
        lanes = slice(c * HD, (c + 1) * HD)
        slab = column_in[...].astype(F32).reshape(PART, TOK)[c * HD : (c + 1) * HD, :]
        middle[:, lanes] = (res_ref[:, lanes].astype(F32) + jnp.transpose(slab)).astype(BF16)

    outgoing[...] = (
        nn(chosen_rows[...], middle[...]).astype(BF16).reshape(NSEQ, CAP, PART)
    )

    def my_rows(index):
        return pl.ds(pl.multiple_of(index * CAP, CAP), CAP)

    x_up = lax.rem(xi + 1, NX) * 2 + core
    x_down = lax.rem(xi + NX - 1, NX) * 2 + core
    x_far = lax.rem(xi + 2, NX) * 2 + core

    def half_rows(index, side):
        start = index * GROWS + side * (GROWS // 2)
        return pl.ds(pl.multiple_of(start, GROWS // 2), GROWS // 2)

    def group_rows(index):
        return pl.ds(pl.multiple_of(index * GROWS, GROWS), GROWS)

    @pl.loop(1, NSEQ)
    def _(n):
        to = lax.rem(group + turn(n // GSRC), NG) * GSRC + lax.rem(me + n, GSRC)
        remote(
            outgoing.at[to],
            rows_in.at[hd, my_rows(me)],
            s_disp,
            r_disp.at[group],
            seq=to,
        ).start()

    rows_in[hd, my_rows(me), :] = outgoing[me]

    def gather(i):
        g = lax.rem(group + NG - turn(i), NG)
        part = group_rows(g)

        @pl.when(i == 0)
        def _():
            remote(
                outgoing.at[0 : GSRC - 1],
                outgoing.at[0 : GSRC - 1],
                s_disp,
                r_disp.at[g],
                seq=me,
            ).wait_recv()

        @pl.when(i > 0)
        def _():
            remote(
                outgoing.at[0:GSRC], outgoing.at[0:GSRC], s_disp, r_disp.at[g], seq=me
            ).wait_recv()

        block = rows_in.at[hd, part]
        remote(block, block, s_gath, r_gath.at[g, 0], head=x_up).start()
        remote(block, block, s_gath, r_gath.at[g, 1], head=x_down).start()
        remote(block, block, s_fwd, r_fwd.at[g], head=partner).start()

    def forward(i):
        g = lax.rem(group + NG - turn(i), NG)
        part = group_rows(g)
        for side, source, to in ((0, x_down, x_up), (1, x_up, x_down)):
            block = rows_in.at[source, part]
            remote(block, block, s_gath, r_gath.at[g, side], head=hd).wait_recv()
            piece = rows_in.at[source, half_rows(g, side)]
            remote(piece, piece, s_gath, r_gath.at[g, 2 + side], head=to).start()
            remote(block, block, s_fwd, r_fwd.at[g], head=partner).start()

    def forward_far(i):
        g = lax.rem(group + NG - turn(i), NG)
        for side in range(2):
            piece = rows_in.at[x_far, half_rows(g, side)]
            remote(piece, piece, s_gath, r_gath.at[g, 2 + side], head=hd).wait_recv()
        block = rows_in.at[x_far, group_rows(g)]
        remote(block, block, s_fwd, r_fwd.at[g], head=partner).start()

    def serve(i):
        g = lax.rem(group + NG - turn(i), NG)
        part = group_rows(g)

        @pl.when(i == 0)
        def _():
            for load in loads:
                load.wait()

        remote(
            rows_in.at[0:NX, 0:GROWS], rows_in.at[0:NX, 0:GROWS], s_fwd, r_fwd.at[g], head=hd
        ).wait_recv()
        squares = jnp.zeros((GROWS, HD), F32)
        for h in range(NHEAD):
            block = rows_in[h, part, :].astype(F32)
            block = block * block
            for c in range(PART // HD):
                squares = squares + block[:, c * HD : (c + 1) * HD]
        scale = lax.rsqrt(jnp.sum(squares, axis=1, keepdims=True) / D + EPSILON)
        for h in range(NHEAD):
            lanes = slice(h * PART, (h + 1) * PART)
            normed[:, lanes] = (
                rows_in[h, part, :].astype(F32) * scale * ng_ref[:, lanes]
            ).astype(BF16)
        gated = nt(normed[...], gate[...])
        upped = nt(normed[...], up[...])
        hidden = (gated / (1.0 + jnp.exp(-gated)) * upped).astype(BF16)
        for h in range(NHEAD):
            lanes = slice(h * PART, (h + 1) * PART)
            result[h % 2, h // 2, part, :] = nn(hidden, down[:, lanes]).astype(BF16)
        remote(
            result.at[1 - core, :, part],
            pair_in.at[:, part],
            s_pair,
            r_pair.at[g],
            head=partner,
        ).start()

    def both_cores(x, rows):
        return result[core, x, rows, :].astype(F32) + pair_in[x, rows, :].astype(F32)

    def reduce_pair(i):
        g = lax.rem(group + NG - turn(i), NG)
        part = group_rows(g)
        remote(
            pair_in.at[:, part], pair_in.at[:, part], s_pair, r_pair.at[g], head=hd
        ).wait_recv()
        far_sum[part, :] = both_cores(x_far // 2, part).astype(BF16)
        for side, to in ((0, x_up), (1, x_down)):
            piece = half_rows(g, side)
            remote(
                far_sum.at[piece],
                ring_in.at[piece],
                s_ring,
                r_ring.at[g, side],
                head=to,
            ).start()

    def reduce_mid(i):
        g = lax.rem(group + NG - turn(i), NG)
        part = group_rows(g)
        for side, to in ((0, x_up), (1, x_down)):
            piece, other = half_rows(g, side), half_rows(g, 1 - side)
            near_sum[side, other, :] = both_cores(to // 2, other).astype(BF16)
            remote(
                ring_in.at[piece], ring_in.at[piece], s_ring, r_ring.at[g, side], head=hd
            ).wait_recv()
            near_sum[side, piece, :] = (
                both_cores(to // 2, piece) + ring_in[piece, :].astype(F32)
            ).astype(BF16)
            remote(
                near_sum.at[side, part],
                plane_in.at[side, part],
                s_plane,
                r_plane.at[g],
                head=to,
            ).start()

    def reduce_plane(i):
        g = lax.rem(group + NG - turn(i), NG)
        part = group_rows(g)
        remote(
            plane_in.at[:, part], plane_in.at[:, part], s_plane, r_plane.at[g], head=hd
        ).wait_recv()
        total = both_cores(xi, part)
        for side in range(2):
            total = total + plane_in[side, part, :].astype(F32)
        summed[part, :] = total.astype(BF16)

        @pl.loop(0, GSRC)
        def _(j):
            to = g * GSRC + j

            @pl.when(to != me)
            def _():
                remote(
                    summed.at[my_rows(to)], returned.at[my_rows(me)], s_ret, r_ret, seq=to
                ).start()

    stages = (
        gather,
        forward,
        forward_far,
        serve,
        reduce_pair,
        reduce_mid,
        reduce_plane,
    )

    def step(t, carry):
        for number, stage in enumerate(stages):
            pl.when((t >= number) & (t < number + NG))(
                functools.partial(stage, t - number)
            )
        return carry

    lax.fori_loop(0, NG + len(stages) - 1, step, 0)
    returned[my_rows(me), :] = summed[my_rows(me), :]

    slots = (NSEQ - 1) * CAP
    remote(
        returned.at[0:slots], returned.at[0:slots], s_ret, r_ret, seq=me
    ).wait_recv()
    for c in range(PART // HD):
        lanes = slice(c * HD, (c + 1) * HD)
        out_ref[:, lanes] = (
            middle[:, lanes].astype(F32)
            + (
                nn(picks[0], returned[:, lanes]) * mixes[0]
                + nn(picks[1], returned[:, lanes]) * mixes[1]
            )
        ).astype(BF16)

    remote(
        outgoing.at[0 : NSEQ - 1], outgoing.at[0 : NSEQ - 1], s_disp, r_disp.at[0], seq=me
    ).wait_send()
    remote(
        rows_in.at[0 : NX - 1], rows_in.at[0 : NX - 1], s_gath, r_gath.at[0, 0], head=hd
    ).wait_send()
    remote(rows_in.at[0:NX], rows_in.at[0:NX], s_fwd, r_fwd.at[0], head=hd).wait_send()
    remote(pair_in, pair_in, s_pair, r_pair.at[0], head=hd).wait_send()
    remote(far_sum, far_sum, s_ring, r_ring.at[0, 0], head=hd).wait_send()
    remote(plane_in, plane_in, s_plane, r_plane.at[0], head=hd).wait_send()
    remote(
        returned.at[0:slots], returned.at[0:slots], s_ret, r_ret, seq=me
    ).wait_send()
    remote(
        own_state.at[0:others], all_state.at[0:others], s_state, r_state, seq=me
    ).wait_send()
    remote(
        all_info.at[0:others], all_info.at[0:others], s_info, r_info, seq=me
    ).wait_send()
    remote(
        own_carry.at[0:others], all_carry.at[0:others], s_carry, r_carry, seq=me
    ).wait_send()
    remote(attended.at[0:3], attended.at[0:3], s_att, r_att.at[0, 0], seq=me).wait_send()
    w_copy(pl.ds(0, (NZ - 1) * WCOLS), 0, me, 0).wait_send()
    remote(paired, paired, s_pp, r_pp.at[0], head=hd).wait_send()
    remote(
        arrived.at[:, 0 : NX - 1],
        arrived.at[:, 0 : NX - 1],
        s_part,
        r_part.at[0],
        head=hd,
    ).wait_send()
    remote(
        column_in.at[0 : NY - 1], column_in.at[0 : NY - 1], s_col, r_col, seq=me
    ).wait_send()


def layer(*operands):
    vmem = pl.BlockSpec(memory_space=pltpu.VMEM)
    anywhere = pl.BlockSpec(memory_space=pl.ANY)
    dma = pltpu.SemaphoreType.DMA
    return pl.pallas_call(
        layer_kernel,
        out_shape=jax.ShapeDtypeStruct((TOK, PART), BF16),
        in_specs=[vmem] * 11 + [anywhere] * 3,
        out_specs=vmem,
        scratch_shapes=[
            pltpu.VMEM((HEADS, TOK), F32),
            pltpu.VMEM((NSEQ, 32, HD), BF16),
            pltpu.VMEM((HEADS, 1, TOK), F32),
            pltpu.VMEM((NSEQ, 32, HD), BF16),
            pltpu.VMEM((NSEQ, 1, TOK), F32),
            pltpu.VMEM((NSEQ, 32, HD), BF16),
            pltpu.VMEM((NSEQ, 32, HD), BF16),
            pltpu.VMEM((TOK, HEADS * HD), F32),
            pltpu.VMEM((NY, TOK, HEADS * HD), BF16),
            pltpu.VMEM((NZ * WCOLS, HEADS * HD), BF16),
            pltpu.VMEM((NY, NX, 2, WCOLS, TOK), BF16),
            pltpu.VMEM((NY, NX, WCOLS, TOK), BF16),
            pltpu.VMEM((NY, NX, WCOLS, TOK), BF16),
            pltpu.VMEM((NY, NX, WCOLS, TOK), BF16),
            pltpu.VMEM((NY, WCOLS, TOK), BF16),
            pltpu.VMEM((NY, WCOLS, TOK), BF16),
            pltpu.VMEM((TOK, PART), BF16),
            pltpu.VMEM((SLOTS, TOK), BF16),
            pltpu.VMEM((2, TOK, SLOTS), BF16),
            pltpu.VMEM((2, TOK, TOK), F32),
            pltpu.VMEM((FF, D), BF16),
            pltpu.VMEM((FF, D), BF16),
            pltpu.VMEM((FF, D), BF16),
            pltpu.VMEM((NSEQ, CAP, PART), BF16),
            pltpu.VMEM((NHEAD, SLOTS, PART), BF16),
            pltpu.VMEM((GROWS, D), BF16),
            pltpu.VMEM((2, NX, SLOTS, PART), BF16),
            pltpu.VMEM((NX, SLOTS, PART), BF16),
            pltpu.VMEM((SLOTS, PART), BF16),
            pltpu.VMEM((SLOTS, PART), BF16),
            pltpu.VMEM((2, SLOTS, PART), BF16),
            pltpu.VMEM((2, SLOTS, PART), BF16),
            pltpu.VMEM((SLOTS, PART), BF16),
            pltpu.VMEM((SLOTS, PART), BF16),
            dma,
            dma,
            dma,
            dma,
            dma,
            dma,
            dma,
            dma((3, 2)),
            dma,
            dma((2, 4)),
            dma,
            dma((NY,)),
            dma,
            dma((NY,)),
            dma,
            dma,
            dma((3,)),
            dma,
            dma((NG,)),
            dma,
            dma((NG, 4)),
            dma,
            dma((NG,)),
            dma,
            dma((NG,)),
            dma,
            dma((NG, 2)),
            dma,
            dma((NG,)),
            dma,
            dma,
        ],
        compiler_params=pltpu.CompilerParams(
            collective_id=0, has_side_effects=True, vmem_limit_bytes=VMEM_LIMIT
        ),
        name="layer",
    )(*operands)


def shards(
    queries,
    key_vectors,
    value_vectors,
    log_decay,
    doc_ids,
    head_gain,
    output_weight,
    residual,
    norm_gain,
    routing,
    route_weights,
    gate_weight,
    up_weight,
    down_weight,
):
    return layer(
        queries,
        key_vectors,
        value_vectors,
        log_decay.T,
        doc_ids.reshape(1, -1),
        head_gain.reshape(1, -1),
        output_weight.T,
        residual,
        routing.T,
        route_weights.T,
        norm_gain.reshape(1, -1),
        gate_weight[0].T,
        up_weight[0].T,
        down_weight[0],
    )


def solution(mesh):
    in_specs = (
        P("seq", "head"),
        P("seq", "head"),
        P("seq", "head"),
        P("seq", "head"),
        P("seq"),
        P("head"),
        P("head", "seq"),
        P("seq", "head"),
        P(),
        P("seq", None),
        P("seq", None),
        P("seq", None, "head"),
        P("seq", None, "head"),
        P("seq", "head", None),
    )
    return jax.shard_map(
        shards, mesh=mesh, in_specs=in_specs, out_specs=P("seq", "head"), check_vma=False
    )
```

```python
import functools

import jax
import jax.numpy as jnp
from jax import lax
from jax.experimental import pallas as pl
from jax.experimental.pallas import tpu as pltpu
from jax.sharding import PartitionSpec as P

MESH = pl.DeviceIdType.MESH
F32, BF16 = jnp.float32, jnp.bfloat16
EPSILON = 1e-06
NZ, NY, NX = 8, 4, 4
NSEQ, NHEAD = NZ * NY, 2 * NX
TOK, HEADS, HD = 128, 8, 128
WCOLS = 96
PART = 384
D = PART * NHEAD
CAP = 16
NG = 4
GSRC = NSEQ // NG
GROWS = GSRC * CAP
SLOTS = NSEQ * CAP
FF = 576
VMEM_LIMIT = 60 * 1024 * 1024


def nt(a, b):
    return lax.dot_general(a, b, (((1,), (1,)), ((), ())), preferred_element_type=F32)


def nn(a, b):
    return jnp.dot(a, b, preferred_element_type=F32)


def remote(src, dst, send_sem, recv_sem, **device):
    return pltpu.make_async_remote_copy(
        src_ref=src,
        dst_ref=dst,
        send_sem=send_sem,
        recv_sem=recv_sem,
        device_id=device,
        device_id_type=MESH,
    )


def greet(me, hd):
    barrier = pltpu.get_barrier_semaphore()

    @pl.loop(1, NSEQ)
    def _(d):
        pl.semaphore_signal(
            barrier, inc=1, device_id={"seq": lax.rem(me + d, NSEQ)}, device_id_type=MESH
        )

    @pl.loop(1, NHEAD)
    def _(d):
        pl.semaphore_signal(
            barrier, inc=1, device_id={"head": lax.rem(hd + d, NHEAD)}, device_id_type=MESH
        )

    return barrier


def turn(i):
    return i + i // 2 - 2 * (i // 3)


def around(n):
    return (n + 1) // 2 * (2 * lax.rem(n, 2) - 1)


def columns(row):
    return jnp.transpose(jnp.broadcast_to(row, (TOK, TOK)))


def layer_kernel(
    q_hbm,
    k_hbm,
    v_hbm,
    ld_hbm,
    doc_hbm,
    hg_hbm,
    w_hbm,
    res_hbm,
    rout_hbm,
    mix_hbm,
    ng_hbm,
    gate_hbm,
    up_hbm,
    down_hbm,
    out_ref,
    q_ref,
    k_ref,
    v_ref,
    ld_ref,
    doc_ref,
    hg_ref,
    res_ref,
    rout_ref,
    mix_ref,
    ng_ref,
    decay,
    reaches,
    own_state,
    own_info,
    all_state,
    all_info,
    own_carry,
    all_carry,
    inner,
    attended,
    weight,
    partial,
    paired,
    half_sum,
    arrived,
    column_out,
    column_in,
    middle,
    chosen_rows,
    picks,
    mixes,
    gate,
    up,
    down,
    outgoing,
    rows_in,
    normed,
    result,
    pair_in,
    far_sum,
    ring_in,
    near_sum,
    plane_in,
    summed,
    returned,
    s_state,
    r_state,
    s_info,
    r_info,
    s_carry,
    r_carry,
    s_att,
    r_att,
    s_w,
    r_w,
    s_pp,
    r_pp,
    s_part,
    r_part,
    s_col,
    r_col,
    s_load,
    s_in,
    s_disp,
    r_disp,
    s_gath,
    r_gath,
    s_fwd,
    r_fwd,
    s_pair,
    r_pair,
    s_ring,
    r_ring,
    s_plane,
    r_plane,
    s_ret,
    r_ret,
):
    me, hd = lax.axis_index("seq"), lax.axis_index("head")
    zi, yi = me // NY, lax.rem(me, NY)
    xi, core = hd // 2, lax.rem(hd, 2)
    partner = xi * 2 + 1 - core
    group = me // GSRC
    barrier = greet(me, hd)
    loads = [
        pltpu.make_async_copy(gate_hbm, gate, s_load.at[0]),
        pltpu.make_async_copy(up_hbm, up, s_load.at[1]),
        pltpu.make_async_copy(down_hbm, down, s_load.at[2]),
    ]

    def w_rows(z, start=0, size=WCOLS):
        return pl.ds(pl.multiple_of(lax.rem(z + NZ, NZ) * WCOLS + start, 16), size)

    fetches = [
        pltpu.make_async_copy(source, target, s_in.at[n])
        for n, (source, target) in enumerate(
            (
                (ld_hbm, ld_ref),
                (doc_hbm, doc_ref),
                (k_hbm, k_ref),
                (v_hbm, v_ref),
                (w_hbm, weight.at[w_rows(zi)]),
                (q_hbm, q_ref),
                (rout_hbm, rout_ref),
                (mix_hbm, mix_ref),
                (hg_hbm, hg_ref),
                (res_hbm, res_ref),
                (ng_hbm, ng_ref),
            )
        )
    ]
    for fetch in fetches:
        fetch.start()
    for load in loads:
        load.start()
    for fetch in fetches[0:4]:
        fetch.wait()

    rows = lax.broadcasted_iota(jnp.int32, (TOK, TOK), 0)
    cols = lax.broadcasted_iota(jnp.int32, (TOK, TOK), 1)
    upper = (rows <= cols).astype(F32)
    sums = jnp.dot(
        ld_ref[...], upper, preferred_element_type=F32, precision=lax.Precision.HIGHEST
    )
    decay[...] = sums
    last = sums[:, TOK - 1 : TOK]
    doc = doc_ref[...].astype(F32)
    doc_first, doc_last = doc[:, 0:1], doc[:, TOK - 1 : TOK]
    tail = jnp.exp(last - sums) * (doc == doc_last).astype(F32)
    gain = jnp.exp(last) * (doc_first == doc_last).astype(F32)
    lane = lax.broadcasted_iota(jnp.int32, (HEADS, TOK), 1)
    info = jnp.where(lane < 32, gain, jnp.where(lane < 64, doc_first, doc_last))
    for h in range(HEADS):
        own_info[h] = info[h : h + 1, :]
    for h in range(HEADS):
        lanes = slice(h * HD, (h + 1) * HD)
        key_t = jnp.transpose(k_ref[:, lanes].astype(F32))
        state = nn((key_t * tail[h : h + 1, :]).astype(BF16), v_ref[:, lanes])
        own_state[4 * h : 4 * h + 4] = state.astype(BF16).reshape(4, 32, HD)

    pl.semaphore_wait(barrier, NSEQ + NHEAD - 2)

    @pl.loop(1, NSEQ)
    def _(n):
        to = lax.rem(me + NSEQ + around(n), NSEQ)
        remote(own_info.at[to // 4], all_info.at[me], s_info, r_info, seq=to).start()
        remote(own_state.at[to], all_state.at[me], s_state, r_state, seq=to).start()

    all_state[me] = own_state[me]
    all_info[me] = own_info[me // 4]

    right = lax.rem(zi + 1, NZ) * NY + yi
    left = lax.rem(zi + NZ - 1, NZ) * NY + yi
    half = WCOLS // 2

    def w_copy(rows, k, to, side):
        block = weight.at[rows]
        return remote(block, block, s_w, r_w.at[side, k], seq=to)

    def w_step(k):
        w_copy(w_rows(zi - 1 - k), k, me, 0).wait_recv()
        from_left = w_rows(zi - 1 - k) if k < 2 else w_rows(zi - 1 - k, 0, half)
        w_copy(from_left, k + 1, right, 0).start()
        w_copy(w_rows(zi + 1 + k), k, me, 1).wait_recv()
        from_right = w_rows(zi + 1 + k) if k < 2 else w_rows(zi + 1 + k, half, half)
        w_copy(from_right, k + 1, left, 1).start()

    fetches[4].wait()
    w_copy(w_rows(zi), 0, right, 0).start()
    w_copy(w_rows(zi), 0, left, 1).start()
    for fetch in fetches[5:]:
        fetch.wait()

    doc_rows = jnp.broadcast_to(doc, (TOK, TOK))
    kept = (cols <= rows) & (jnp.transpose(doc_rows) == doc_rows)
    for h in range(HEADS):
        lanes = slice(h * HD, (h + 1) * HD)
        decay_row = jnp.broadcast_to(decay[h : h + 1, :], (TOK, TOK))
        gap = jnp.transpose(decay_row) - decay_row
        factor = jnp.where(kept, jnp.exp(jnp.minimum(gap, 0.0)), 0.0)
        weighted = (nt(q_ref[:, lanes], k_ref[:, lanes]) * factor).astype(BF16)
        inner[:, lanes] = nn(weighted, v_ref[:, lanes])
    expert = lax.broadcasted_iota(jnp.int32, (NSEQ, TOK), 0)
    hits = [(expert == rout_ref[j : j + 1, :]).astype(F32) for j in range(2)]
    earlier = (
        lax.broadcasted_iota(jnp.int32, (TOK, TOK), 0)
        < lax.broadcasted_iota(jnp.int32, (TOK, TOK), 1)
    ).astype(BF16)
    count = nn((hits[0] + hits[1]).astype(BF16), earlier)
    places = [
        rout_ref[j : j + 1, :].astype(F32) * CAP
        + jnp.sum(hits[j] * count, axis=0, keepdims=True)
        for j in range(2)
    ]
    slot = lax.broadcasted_iota(jnp.int32, (NSEQ * CAP, TOK), 0).astype(F32)
    chosen = (slot == places[0]).astype(F32) + (slot == places[1]).astype(F32)
    chosen_rows[...] = chosen.astype(BF16)
    lane = lax.broadcasted_iota(jnp.int32, (TOK, NSEQ * CAP), 1).astype(F32)
    for j in range(2):
        picks[j] = (lane == columns(places[j])[:, 0:1]).astype(BF16)
        mixes[j] = columns(mix_ref[j : j + 1, :])


    others = NSEQ - 1
    remote(
        own_state.at[0:others], all_state.at[0:others], s_state, r_state, seq=me
    ).wait_recv()
    remote(
        all_info.at[0:others], all_info.at[0:others], s_info, r_info, seq=me
    ).wait_recv()

    carried, before = jnp.zeros((32, HD), F32), jnp.full((1, 1), -1.0, F32)
    for b in range(NSEQ):
        own_carry[b] = carried.astype(BF16)
        row = all_info[b]
        through = jnp.where(row[:, 32:33] == before, row[:, 0:1], 0.0)
        carried, before = all_state[b].astype(F32) + through * carried, row[:, 64:65]

    @pl.loop(1, NSEQ)
    def _(n):
        to = lax.rem(me + NSEQ + around(n), NSEQ)
        remote(
            own_carry.at[to], all_carry.at[me], s_carry, r_carry.at[me // 16], seq=to
        ).start()

    all_carry[me] = own_carry[me]
    before_doc = all_info[jnp.maximum(me - 1, 0)][:, 64:65]
    before_doc = jnp.where(jnp.full((1, 1), me, jnp.int32) == 0, -1.0, before_doc)
    w_step(0)
    reaches[...] = jnp.exp(decay[...]) * (doc == before_doc).astype(F32)
    y_up = zi * NY + lax.rem(yi + 1, NY)
    y_down = zi * NY + lax.rem(yi + NY - 1, NY)
    near = me // 16

    def half_lanes(part):
        return pl.ds(pl.multiple_of(part * 512, 512), 512)

    def att_half(y, part):
        return attended.at[lax.rem(y + NY, NY), :, half_lanes(part)]

    def att_wait(block, side, part):
        remote(block, block, s_att, r_att.at[side, part], seq=me).wait_recv()

    for order in range(2):
        part = near if order == 0 else 1 - near
        slabs = own_carry.at[0 : 15 if order == 0 else 16]
        remote(slabs, slabs, s_carry, r_carry.at[part], seq=me).wait_recv()
        for j in range(4):
            h = part * 4 + j
            lanes = pl.ds(pl.multiple_of(h * HD, HD), HD)
            carried = all_carry[pl.ds(4 * h, 4)].reshape(HD, HD)
            raw = inner[:, lanes] + nn(q_ref[:, lanes], carried) * columns(
                reaches[pl.ds(h, 1), :]
            )
            scale = lax.rsqrt(jnp.mean(raw * raw, axis=1, keepdims=True) + EPSILON)
            attended[yi, :, lanes] = (raw * scale * hg_ref[:, lanes]).astype(BF16)
            if j % 2 == 1:
                pair = pl.ds(pl.multiple_of((h - 1) * HD, 2 * HD), 2 * HD)
                block = attended.at[yi, :, pair]
                remote(block, block, s_att, r_att.at[0, order], seq=y_up).start()
                remote(block, block, s_att, r_att.at[1, order], seq=y_down).start()
        if order == 0:
            w_step(1)

    block = att_half(yi - 1, near)
    att_wait(block, 0, 0)
    remote(block, block, s_att, r_att.at[2, 0], seq=y_up).start()
    w_step(2)
    block = att_half(yi + 1, 1 - near)
    att_wait(block, 1, 1)
    remote(block, block, s_att, r_att.at[2, 1], seq=y_down).start()
    w_copy(w_rows(zi + 4, 0, half), 3, me, 0).wait_recv()
    w_copy(w_rows(zi + 4, half, half), 3, me, 1).wait_recv()

    def project(i):
        y = lax.rem(yi + NY - turn(i), NY)
        pl.when(i == 1)(lambda: att_wait(att_half(yi - 1, 1 - near), 0, 1))
        pl.when(i == 2)(lambda: att_wait(att_half(yi + 1, near), 1, 0))

        @pl.when(i == 3)
        def _():
            att_wait(att_half(yi + 2, near), 2, 0)
            att_wait(att_half(yi + 2, 1 - near), 2, 1)

        partial[y] = nt(weight[...], attended[y]).astype(BF16).reshape(NX, 2, WCOLS, TOK)
        remote(
            partial.at[y, :, 1 - core], paired.at[y], s_pp, r_pp.at[y], head=partner
        ).start()

    def pair_sum(i):
        y = lax.rem(yi + NY - turn(i), NY)
        remote(paired.at[y], paired.at[y], s_pp, r_pp.at[y], head=hd).wait_recv()
        for d in (2, 1, 3, 0):
            x = lax.rem(xi + d, NX)
            both = (
                partial[y, x, core].astype(F32) + paired[y, x].astype(F32)
            ).astype(BF16)
            if d:
                half_sum[y, x] = both
                remote(
                    half_sum.at[y, x],
                    arrived.at[y, xi],
                    s_part,
                    r_part.at[y],
                    head=x * 2 + core,
                ).start()
            else:
                arrived[y, xi] = both

    def plane_sum(i):
        y = lax.rem(yi + NY - turn(i), NY)
        remote(
            arrived.at[y, 0 : NX - 1],
            arrived.at[y, 0 : NX - 1],
            s_part,
            r_part.at[y],
            head=hd,
        ).wait_recv()
        total = arrived[y, 0].astype(F32)
        for x in range(1, NX):
            total = total + arrived[y, x].astype(F32)
        column_out[y] = total.astype(BF16)

        @pl.when(i > 0)
        def _():
            remote(
                column_out.at[y], column_in.at[yi], s_col, r_col, seq=zi * NY + y
            ).start()

        @pl.when(i == 0)
        def _():
            column_in[yi] = total.astype(BF16)

    def project_step(t, carry):
        pl.when(t < NY)(lambda: project(t))
        pl.when(t >= 1)(lambda: pair_sum(t - 1))
        return carry

    lax.fori_loop(0, NY + 1, project_step, 0)
    pl.loop(0, NY)(plane_sum)
    remote(
        column_in.at[0 : NY - 1], column_in.at[0 : NY - 1], s_col, r_col, seq=me
    ).wait_recv()
    for c in range(PART // HD):
        lanes = slice(c * HD, (c + 1) * HD)
        slab = column_in[...].astype(F32).reshape(PART, TOK)[c * HD : (c + 1) * HD, :]
        middle[:, lanes] = (res_ref[:, lanes].astype(F32) + jnp.transpose(slab)).astype(BF16)

    outgoing[...] = (
        nn(chosen_rows[...], middle[...]).astype(BF16).reshape(NSEQ, CAP, PART)
    )

    def my_rows(index):
        return pl.ds(pl.multiple_of(index * CAP, CAP), CAP)

    x_up = lax.rem(xi + 1, NX) * 2 + core
    x_down = lax.rem(xi + NX - 1, NX) * 2 + core
    x_far = lax.rem(xi + 2, NX) * 2 + core

    def half_rows(index, side):
        start = index * GROWS + side * (GROWS // 2)
        return pl.ds(pl.multiple_of(start, GROWS // 2), GROWS // 2)

    def group_rows(index):
        return pl.ds(pl.multiple_of(index * GROWS, GROWS), GROWS)

    @pl.loop(1, NSEQ)
    def _(n):
        to = lax.rem(group + turn(n // GSRC), NG) * GSRC + lax.rem(me + n, GSRC)
        remote(
            outgoing.at[to],
            rows_in.at[hd, my_rows(me)],
            s_disp,
            r_disp.at[group],
            seq=to,
        ).start()

    rows_in[hd, my_rows(me), :] = outgoing[me]

    def gather(i):
        g = lax.rem(group + NG - turn(i), NG)
        part = group_rows(g)

        blocks = outgoing.at[0 : GSRC - 1 if i == 0 else GSRC]
        remote(blocks, blocks, s_disp, r_disp.at[g], seq=me).wait_recv()
        block = rows_in.at[hd, part]
        remote(block, block, s_gath, r_gath.at[g, 0], head=x_up).start()
        remote(block, block, s_gath, r_gath.at[g, 1], head=x_down).start()
        remote(block, block, s_fwd, r_fwd.at[g], head=partner).start()

    def forward(i):
        g = lax.rem(group + NG - turn(i), NG)
        part = group_rows(g)
        for side, source, to in ((0, x_down, x_up), (1, x_up, x_down)):
            block = rows_in.at[source, part]
            remote(block, block, s_gath, r_gath.at[g, side], head=hd).wait_recv()
            piece = rows_in.at[source, half_rows(g, side)]
            remote(piece, piece, s_gath, r_gath.at[g, 2 + side], head=to).start()
            remote(block, block, s_fwd, r_fwd.at[g], head=partner).start()

    def forward_far(i):
        g = lax.rem(group + NG - turn(i), NG)
        for side in range(2):
            piece = rows_in.at[x_far, half_rows(g, side)]
            remote(piece, piece, s_gath, r_gath.at[g, 2 + side], head=hd).wait_recv()
        block = rows_in.at[x_far, group_rows(g)]
        remote(block, block, s_fwd, r_fwd.at[g], head=partner).start()

    def serve(i):
        g = lax.rem(group + NG - turn(i), NG)
        part = group_rows(g)

        if i == 0:
            for load in loads:
                load.wait()
        remote(
            rows_in.at[0:NX, 0:GROWS], rows_in.at[0:NX, 0:GROWS], s_fwd, r_fwd.at[g], head=hd
        ).wait_recv()
        squares = jnp.zeros((GROWS, HD), F32)
        for h in range(NHEAD):
            block = rows_in[h, part, :].astype(F32)
            block = block * block
            for c in range(PART // HD):
                squares = squares + block[:, c * HD : (c + 1) * HD]
        scale = lax.rsqrt(jnp.sum(squares, axis=1, keepdims=True) / D + EPSILON)
        for h in range(NHEAD):
            lanes = slice(h * PART, (h + 1) * PART)
            normed[:, lanes] = (
                rows_in[h, part, :].astype(F32) * scale * ng_ref[:, lanes]
            ).astype(BF16)
        gated = nt(normed[...], gate[...])
        upped = nt(normed[...], up[...])
        hidden = (gated / (1.0 + jnp.exp(-gated)) * upped).astype(BF16)
        for h in range(NHEAD):
            lanes = slice(h * PART, (h + 1) * PART)
            result[h % 2, h // 2, part, :] = nn(hidden, down[:, lanes]).astype(BF16)
        remote(
            result.at[1 - core, :, part],
            pair_in.at[:, part],
            s_pair,
            r_pair.at[g],
            head=partner,
        ).start()

    def both_cores(x, rows):
        return result[core, x, rows, :].astype(F32) + pair_in[x, rows, :].astype(F32)

    def reduce_pair(i):
        g = lax.rem(group + NG - turn(i), NG)
        part = group_rows(g)
        remote(
            pair_in.at[:, part], pair_in.at[:, part], s_pair, r_pair.at[g], head=hd
        ).wait_recv()
        far_sum[part, :] = both_cores(x_far // 2, part).astype(BF16)
        for side, to in ((0, x_up), (1, x_down)):
            piece = half_rows(g, side)
            remote(
                far_sum.at[piece],
                ring_in.at[piece],
                s_ring,
                r_ring.at[g, side],
                head=to,
            ).start()

    def reduce_mid(i):
        g = lax.rem(group + NG - turn(i), NG)
        part = group_rows(g)
        for side, to in ((0, x_up), (1, x_down)):
            piece, other = half_rows(g, side), half_rows(g, 1 - side)
            near_sum[side, other, :] = both_cores(to // 2, other).astype(BF16)
            remote(
                ring_in.at[piece], ring_in.at[piece], s_ring, r_ring.at[g, side], head=hd
            ).wait_recv()
            near_sum[side, piece, :] = (
                both_cores(to // 2, piece) + ring_in[piece, :].astype(F32)
            ).astype(BF16)
            remote(
                near_sum.at[side, part],
                plane_in.at[side, part],
                s_plane,
                r_plane.at[g],
                head=to,
            ).start()

    def reduce_plane(i):
        g = lax.rem(group + NG - turn(i), NG)
        part = group_rows(g)
        remote(
            plane_in.at[:, part], plane_in.at[:, part], s_plane, r_plane.at[g], head=hd
        ).wait_recv()
        total = both_cores(xi, part)
        for side in range(2):
            total = total + plane_in[side, part, :].astype(F32)
        summed[part, :] = total.astype(BF16)

        @pl.loop(0, GSRC)
        def _(j):
            to = g * GSRC + j

            @pl.when(to != me)
            def _():
                remote(
                    summed.at[my_rows(to)], returned.at[my_rows(me)], s_ret, r_ret, seq=to
                ).start()

    for stage, i in (
        (gather, 0),
        (gather, 1),
        (forward, 0),
        (gather, 2),
        (forward, 1),
        (forward_far, 0),
        (gather, 3),
        (serve, 0),
        (forward, 2),
        (forward_far, 1),
        (forward, 3),
        (serve, 1),
        (reduce_pair, 0),
        (forward_far, 2),
        (forward_far, 3),
        (serve, 2),
        (reduce_pair, 1),
        (reduce_mid, 0),
        (serve, 3),
        (reduce_pair, 2),
        (reduce_mid, 1),
        (reduce_pair, 3),
        (reduce_plane, 0),
        (reduce_mid, 2),
        (reduce_plane, 1),
        (reduce_mid, 3),
        (reduce_plane, 2),
        (reduce_plane, 3),
    ):
        stage(i)
    returned[my_rows(me), :] = summed[my_rows(me), :]

    slots = (NSEQ - 1) * CAP
    remote(
        returned.at[0:slots], returned.at[0:slots], s_ret, r_ret, seq=me
    ).wait_recv()
    for c in range(PART // HD):
        lanes = slice(c * HD, (c + 1) * HD)
        out_ref[:, lanes] = (
            middle[:, lanes].astype(F32)
            + (
                nn(picks[0], returned[:, lanes]) * mixes[0]
                + nn(picks[1], returned[:, lanes]) * mixes[1]
            )
        ).astype(BF16)

    remote(
        outgoing.at[0 : NSEQ - 1], outgoing.at[0 : NSEQ - 1], s_disp, r_disp.at[0], seq=me
    ).wait_send()
    remote(
        rows_in.at[0 : NX - 1], rows_in.at[0 : NX - 1], s_gath, r_gath.at[0, 0], head=hd
    ).wait_send()
    remote(rows_in.at[0:NX], rows_in.at[0:NX], s_fwd, r_fwd.at[0], head=hd).wait_send()
    remote(pair_in, pair_in, s_pair, r_pair.at[0], head=hd).wait_send()
    remote(far_sum, far_sum, s_ring, r_ring.at[0, 0], head=hd).wait_send()
    remote(plane_in, plane_in, s_plane, r_plane.at[0], head=hd).wait_send()
    remote(
        returned.at[0:slots], returned.at[0:slots], s_ret, r_ret, seq=me
    ).wait_send()
    remote(
        own_state.at[0:others], all_state.at[0:others], s_state, r_state, seq=me
    ).wait_send()
    remote(
        all_info.at[0:others], all_info.at[0:others], s_info, r_info, seq=me
    ).wait_send()
    remote(
        own_carry.at[0:others], all_carry.at[0:others], s_carry, r_carry.at[0], seq=me
    ).wait_send()
    remote(attended.at[0:3], attended.at[0:3], s_att, r_att.at[0, 0], seq=me).wait_send()
    w_copy(pl.ds(0, (NZ - 1) * WCOLS), 0, me, 0).wait_send()
    remote(paired, paired, s_pp, r_pp.at[0], head=hd).wait_send()
    remote(
        arrived.at[:, 0 : NX - 1],
        arrived.at[:, 0 : NX - 1],
        s_part,
        r_part.at[0],
        head=hd,
    ).wait_send()
    remote(
        column_in.at[0 : NY - 1], column_in.at[0 : NY - 1], s_col, r_col, seq=me
    ).wait_send()


def layer(*operands):
    vmem = pl.BlockSpec(memory_space=pltpu.VMEM)
    anywhere = pl.BlockSpec(memory_space=pl.ANY)
    dma = pltpu.SemaphoreType.DMA
    return pl.pallas_call(
        layer_kernel,
        out_shape=jax.ShapeDtypeStruct((TOK, PART), BF16),
        in_specs=[anywhere] * 14,
        out_specs=vmem,
        scratch_shapes=[
            pltpu.VMEM((TOK, HEADS * HD), BF16),
            pltpu.VMEM((TOK, HEADS * HD), BF16),
            pltpu.VMEM((TOK, HEADS * HD), BF16),
            pltpu.VMEM((HEADS, TOK), F32),
            pltpu.VMEM((1, TOK), jnp.int32),
            pltpu.VMEM((1, HEADS * HD), F32),
            pltpu.VMEM((TOK, PART), BF16),
            pltpu.VMEM((2, TOK), jnp.int32),
            pltpu.VMEM((2, TOK), F32),
            pltpu.VMEM((1, D), F32),
            pltpu.VMEM((HEADS, TOK), F32),
            pltpu.VMEM((HEADS, TOK), F32),
            pltpu.VMEM((NSEQ, 32, HD), BF16),
            pltpu.VMEM((HEADS, 1, TOK), F32),
            pltpu.VMEM((NSEQ, 32, HD), BF16),
            pltpu.VMEM((NSEQ, 1, TOK), F32),
            pltpu.VMEM((NSEQ, 32, HD), BF16),
            pltpu.VMEM((NSEQ, 32, HD), BF16),
            pltpu.VMEM((TOK, HEADS * HD), F32),
            pltpu.VMEM((NY, TOK, HEADS * HD), BF16),
            pltpu.VMEM((NZ * WCOLS, HEADS * HD), BF16),
            pltpu.VMEM((NY, NX, 2, WCOLS, TOK), BF16),
            pltpu.VMEM((NY, NX, WCOLS, TOK), BF16),
            pltpu.VMEM((NY, NX, WCOLS, TOK), BF16),
            pltpu.VMEM((NY, NX, WCOLS, TOK), BF16),
            pltpu.VMEM((NY, WCOLS, TOK), BF16),
            pltpu.VMEM((NY, WCOLS, TOK), BF16),
            pltpu.VMEM((TOK, PART), BF16),
            pltpu.VMEM((SLOTS, TOK), BF16),
            pltpu.VMEM((2, TOK, SLOTS), BF16),
            pltpu.VMEM((2, TOK, TOK), F32),
            pltpu.VMEM((FF, D), BF16),
            pltpu.VMEM((FF, D), BF16),
            pltpu.VMEM((FF, D), BF16),
            pltpu.VMEM((NSEQ, CAP, PART), BF16),
            pltpu.VMEM((NHEAD, SLOTS, PART), BF16),
            pltpu.VMEM((GROWS, D), BF16),
            pltpu.VMEM((2, NX, SLOTS, PART), BF16),
            pltpu.VMEM((NX, SLOTS, PART), BF16),
            pltpu.VMEM((SLOTS, PART), BF16),
            pltpu.VMEM((SLOTS, PART), BF16),
            pltpu.VMEM((2, SLOTS, PART), BF16),
            pltpu.VMEM((2, SLOTS, PART), BF16),
            pltpu.VMEM((SLOTS, PART), BF16),
            pltpu.VMEM((SLOTS, PART), BF16),
            dma,
            dma,
            dma,
            dma,
            dma,
            dma((2,)),
            dma,
            dma((3, 2)),
            dma,
            dma((2, 4)),
            dma,
            dma((NY,)),
            dma,
            dma((NY,)),
            dma,
            dma,
            dma((3,)),
            dma((11,)),
            dma,
            dma((NG,)),
            dma,
            dma((NG, 4)),
            dma,
            dma((NG,)),
            dma,
            dma((NG,)),
            dma,
            dma((NG, 2)),
            dma,
            dma((NG,)),
            dma,
            dma,
        ],
        compiler_params=pltpu.CompilerParams(
            collective_id=0, has_side_effects=True, vmem_limit_bytes=VMEM_LIMIT
        ),
        name="layer",
    )(*operands)


def shards(
    queries,
    key_vectors,
    value_vectors,
    log_decay,
    doc_ids,
    head_gain,
    output_weight,
    residual,
    norm_gain,
    routing,
    route_weights,
    gate_weight,
    up_weight,
    down_weight,
):
    return layer(
        queries,
        key_vectors,
        value_vectors,
        log_decay.T,
        doc_ids.reshape(1, -1),
        head_gain.reshape(1, -1),
        output_weight.T,
        residual,
        routing.T,
        route_weights.T,
        norm_gain.reshape(1, -1),
        gate_weight[0].T,
        up_weight[0].T,
        down_weight[0],
    )


def solution(mesh):
    in_specs = (
        P("seq", "head"),
        P("seq", "head"),
        P("seq", "head"),
        P("seq", "head"),
        P("seq"),
        P("head"),
        P("head", "seq"),
        P("seq", "head"),
        P(),
        P("seq", None),
        P("seq", None),
        P("seq", None, "head"),
        P("seq", None, "head"),
        P("seq", "head", None),
    )
    return jax.shard_map(
        shards, mesh=mesh, in_specs=in_specs, out_specs=P("seq", "head"), check_vma=False
    )
```

```python
import functools

import jax
import jax.numpy as jnp
from jax import lax
from jax.experimental import pallas as pl
from jax.experimental.pallas import tpu as pltpu
from jax.sharding import PartitionSpec as P

MESH = pl.DeviceIdType.MESH
F32, BF16 = jnp.float32, jnp.bfloat16
EPSILON = 1e-06
NZ, NY, NX = 8, 4, 4
NSEQ, NHEAD = NZ * NY, 2 * NX
TOK, HEADS, HD = 128, 8, 128
WCOLS = 96
PART = 384
D = PART * NHEAD
CAP = 16
NG = 4
GSRC = NSEQ // NG
GROWS = GSRC * CAP
SLOTS = NSEQ * CAP
FF = 576
VMEM_LIMIT = 60 * 1024 * 1024


def nt(a, b):
    return lax.dot_general(a, b, (((1,), (1,)), ((), ())), preferred_element_type=F32)


def nn(a, b):
    return jnp.dot(a, b, preferred_element_type=F32)


def remote(src, dst, send_sem, recv_sem, **device):
    return pltpu.make_async_remote_copy(
        src_ref=src,
        dst_ref=dst,
        send_sem=send_sem,
        recv_sem=recv_sem,
        device_id=device,
        device_id_type=MESH,
    )


def greet(me, hd):
    barrier = pltpu.get_barrier_semaphore()

    @pl.loop(1, NSEQ)
    def _(d):
        pl.semaphore_signal(
            barrier, inc=1, device_id={"seq": lax.rem(me + d, NSEQ)}, device_id_type=MESH
        )

    @pl.loop(1, NHEAD)
    def _(d):
        pl.semaphore_signal(
            barrier, inc=1, device_id={"head": lax.rem(hd + d, NHEAD)}, device_id_type=MESH
        )

    return barrier


def turn(i):
    return i + i // 2 - 2 * (i // 3)


def around(n):
    return (n + 1) // 2 * (2 * lax.rem(n, 2) - 1)


def columns(row):
    return jnp.transpose(jnp.broadcast_to(row, (TOK, TOK)))


def layer_kernel(
    q_hbm,
    k_hbm,
    v_hbm,
    ld_hbm,
    doc_hbm,
    hg_hbm,
    w_hbm,
    res_hbm,
    rout_hbm,
    mix_hbm,
    ng_hbm,
    gate_hbm,
    up_hbm,
    down_hbm,
    out_ref,
    q_ref,
    k_ref,
    v_ref,
    ld_ref,
    doc_ref,
    hg_ref,
    res_ref,
    rout_ref,
    mix_ref,
    ng_ref,
    decay,
    reaches,
    own_state,
    own_info,
    all_state,
    all_info,
    own_carry,
    all_carry,
    inner,
    attended,
    weight,
    partial,
    paired,
    half_sum,
    arrived,
    column_out,
    column_in,
    middle,
    chosen_rows,
    picks,
    mixes,
    gate,
    up,
    down,
    outgoing,
    rows_in,
    normed,
    hidden,
    result,
    pair_in,
    far_sum,
    ring_in,
    near_sum,
    plane_in,
    summed,
    returned,
    s_state,
    r_state,
    s_info,
    r_info,
    s_carry,
    r_carry,
    s_att,
    r_att,
    s_w,
    r_w,
    s_pp,
    r_pp,
    s_part,
    r_part,
    s_col,
    r_col,
    s_load,
    s_in,
    s_disp,
    r_disp,
    s_gath,
    r_gath,
    s_fwd,
    r_fwd,
    s_pair,
    r_pair,
    s_ring,
    r_ring,
    s_plane,
    r_plane,
    s_ret,
    r_ret,
):
    me, hd = lax.axis_index("seq"), lax.axis_index("head")
    zi, yi = me // NY, lax.rem(me, NY)
    xi, core = hd // 2, lax.rem(hd, 2)
    partner = xi * 2 + 1 - core
    group = me // GSRC
    barrier = greet(me, hd)
    loads = [
        pltpu.make_async_copy(gate_hbm, gate, s_load.at[0]),
        pltpu.make_async_copy(up_hbm, up, s_load.at[1]),
        pltpu.make_async_copy(down_hbm, down, s_load.at[2]),
    ]

    def w_rows(z, start=0, size=WCOLS):
        return pl.ds(pl.multiple_of(lax.rem(z + NZ, NZ) * WCOLS + start, 16), size)

    fetches = [
        pltpu.make_async_copy(source, target, s_in.at[n])
        for n, (source, target) in enumerate(
            (
                (ld_hbm, ld_ref),
                (doc_hbm, doc_ref),
                (k_hbm, k_ref),
                (v_hbm, v_ref),
                (w_hbm, weight.at[w_rows(zi)]),
                (q_hbm, q_ref),
                (rout_hbm, rout_ref),
                (mix_hbm, mix_ref),
                (hg_hbm, hg_ref),
                (res_hbm, res_ref),
                (ng_hbm, ng_ref),
            )
        )
    ]
    for fetch in fetches:
        fetch.start()
    for load in loads:
        load.start()
    for fetch in fetches[0:4]:
        fetch.wait()

    rows = lax.broadcasted_iota(jnp.int32, (TOK, TOK), 0)
    cols = lax.broadcasted_iota(jnp.int32, (TOK, TOK), 1)
    upper = (rows <= cols).astype(F32)
    sums = jnp.dot(
        ld_ref[...], upper, preferred_element_type=F32, precision=lax.Precision.HIGHEST
    )
    decay[...] = sums
    last = sums[:, TOK - 1 : TOK]
    doc = doc_ref[...].astype(F32)
    doc_first, doc_last = doc[:, 0:1], doc[:, TOK - 1 : TOK]
    tail = jnp.exp(last - sums) * (doc == doc_last).astype(F32)
    gain = jnp.exp(last) * (doc_first == doc_last).astype(F32)
    lane = lax.broadcasted_iota(jnp.int32, (HEADS, TOK), 1)
    info = jnp.where(lane < 32, gain, jnp.where(lane < 64, doc_first, doc_last))
    for h in range(HEADS):
        own_info[h] = info[h : h + 1, :]
    for h in range(HEADS):
        lanes = slice(h * HD, (h + 1) * HD)
        key_t = jnp.transpose(k_ref[:, lanes].astype(F32))
        state = nn((key_t * tail[h : h + 1, :]).astype(BF16), v_ref[:, lanes])
        own_state[4 * h : 4 * h + 4] = state.astype(BF16).reshape(4, 32, HD)

    pl.semaphore_wait(barrier, NSEQ + NHEAD - 2)

    @pl.loop(1, NSEQ)
    def _(n):
        to = lax.rem(me + NSEQ + around(n), NSEQ)
        remote(own_info.at[to // 4], all_info.at[me], s_info, r_info, seq=to).start()
        remote(own_state.at[to], all_state.at[me], s_state, r_state, seq=to).start()

    all_state[me] = own_state[me]
    all_info[me] = own_info[me // 4]

    right = lax.rem(zi + 1, NZ) * NY + yi
    left = lax.rem(zi + NZ - 1, NZ) * NY + yi
    half = WCOLS // 2

    def w_copy(rows, k, to, side):
        block = weight.at[rows]
        return remote(block, block, s_w, r_w.at[side, k], seq=to)

    def w_step(k):
        w_copy(w_rows(zi - 1 - k), k, me, 0).wait_recv()
        from_left = w_rows(zi - 1 - k) if k < 2 else w_rows(zi - 1 - k, 0, half)
        w_copy(from_left, k + 1, right, 0).start()
        w_copy(w_rows(zi + 1 + k), k, me, 1).wait_recv()
        from_right = w_rows(zi + 1 + k) if k < 2 else w_rows(zi + 1 + k, half, half)
        w_copy(from_right, k + 1, left, 1).start()

    fetches[4].wait()
    w_copy(w_rows(zi), 0, right, 0).start()
    w_copy(w_rows(zi), 0, left, 1).start()
    for fetch in fetches[5:]:
        fetch.wait()

    doc_rows = jnp.broadcast_to(doc, (TOK, TOK))
    kept = (cols <= rows) & (jnp.transpose(doc_rows) == doc_rows)
    for h in range(HEADS):
        lanes = slice(h * HD, (h + 1) * HD)
        decay_row = jnp.broadcast_to(decay[h : h + 1, :], (TOK, TOK))
        gap = jnp.transpose(decay_row) - decay_row
        factor = jnp.where(kept, jnp.exp(jnp.minimum(gap, 0.0)), 0.0)
        weighted = (nt(q_ref[:, lanes], k_ref[:, lanes]) * factor).astype(BF16)
        inner[:, lanes] = nn(weighted, v_ref[:, lanes])
    expert = lax.broadcasted_iota(jnp.int32, (NSEQ, TOK), 0)
    hits = [(expert == rout_ref[j : j + 1, :]).astype(F32) for j in range(2)]
    earlier = (
        lax.broadcasted_iota(jnp.int32, (TOK, TOK), 0)
        < lax.broadcasted_iota(jnp.int32, (TOK, TOK), 1)
    ).astype(BF16)
    count = nn((hits[0] + hits[1]).astype(BF16), earlier)
    places = [
        rout_ref[j : j + 1, :].astype(F32) * CAP
        + jnp.sum(hits[j] * count, axis=0, keepdims=True)
        for j in range(2)
    ]
    slot = lax.broadcasted_iota(jnp.int32, (NSEQ * CAP, TOK), 0).astype(F32)
    chosen = (slot == places[0]).astype(F32) + (slot == places[1]).astype(F32)
    chosen_rows[...] = chosen.astype(BF16)
    lane = lax.broadcasted_iota(jnp.int32, (TOK, NSEQ * CAP), 1).astype(F32)
    for j in range(2):
        picks[j] = (lane == columns(places[j])[:, 0:1]).astype(BF16)
        mixes[j] = columns(mix_ref[j : j + 1, :])


    others = NSEQ - 1
    remote(
        own_state.at[0:others], all_state.at[0:others], s_state, r_state, seq=me
    ).wait_recv()
    remote(
        all_info.at[0:others], all_info.at[0:others], s_info, r_info, seq=me
    ).wait_recv()

    carried, before = jnp.zeros((32, HD), F32), jnp.full((1, 1), -1.0, F32)
    for b in range(NSEQ):
        own_carry[b] = carried.astype(BF16)
        row = all_info[b]
        through = jnp.where(row[:, 32:33] == before, row[:, 0:1], 0.0)
        carried, before = all_state[b].astype(F32) + through * carried, row[:, 64:65]

    @pl.loop(1, NSEQ)
    def _(n):
        to = lax.rem(me + NSEQ + around(n), NSEQ)
        remote(
            own_carry.at[to], all_carry.at[me], s_carry, r_carry.at[me // 16], seq=to
        ).start()

    all_carry[me] = own_carry[me]
    before_doc = all_info[jnp.maximum(me - 1, 0)][:, 64:65]
    before_doc = jnp.where(jnp.full((1, 1), me, jnp.int32) == 0, -1.0, before_doc)
    w_step(0)
    reaches[...] = jnp.exp(decay[...]) * (doc == before_doc).astype(F32)
    y_up = zi * NY + lax.rem(yi + 1, NY)
    y_down = zi * NY + lax.rem(yi + NY - 1, NY)
    near = me // 16

    def half_lanes(part):
        return pl.ds(pl.multiple_of(part * 512, 512), 512)

    def att_half(y, part):
        return attended.at[lax.rem(y + NY, NY), :, half_lanes(part)]

    def att_wait(block, side, part):
        remote(block, block, s_att, r_att.at[side, part], seq=me).wait_recv()

    for order in range(2):
        part = near if order == 0 else 1 - near
        slabs = own_carry.at[0 : 15 if order == 0 else 16]
        remote(slabs, slabs, s_carry, r_carry.at[part], seq=me).wait_recv()
        for j in range(4):
            h = part * 4 + j
            lanes = pl.ds(pl.multiple_of(h * HD, HD), HD)
            carried = all_carry[pl.ds(4 * h, 4)].reshape(HD, HD)
            raw = inner[:, lanes] + nn(q_ref[:, lanes], carried) * columns(
                reaches[pl.ds(h, 1), :]
            )
            scale = lax.rsqrt(jnp.mean(raw * raw, axis=1, keepdims=True) + EPSILON)
            attended[yi, :, lanes] = (raw * scale * hg_ref[:, lanes]).astype(BF16)
            if j % 2 == 1:
                pair = pl.ds(pl.multiple_of((h - 1) * HD, 2 * HD), 2 * HD)
                block = attended.at[yi, :, pair]
                remote(block, block, s_att, r_att.at[0, order], seq=y_up).start()
                remote(block, block, s_att, r_att.at[1, order], seq=y_down).start()
        if order == 0:
            w_step(1)

    block = att_half(yi - 1, near)
    att_wait(block, 0, 0)
    remote(block, block, s_att, r_att.at[2, 0], seq=y_up).start()
    w_step(2)
    block = att_half(yi + 1, 1 - near)
    att_wait(block, 1, 1)
    remote(block, block, s_att, r_att.at[2, 1], seq=y_down).start()
    w_copy(w_rows(zi + 4, 0, half), 3, me, 0).wait_recv()
    w_copy(w_rows(zi + 4, half, half), 3, me, 1).wait_recv()

    def project(i):
        y = lax.rem(yi + NY - turn(i), NY)
        pl.when(i == 1)(lambda: att_wait(att_half(yi - 1, 1 - near), 0, 1))
        pl.when(i == 2)(lambda: att_wait(att_half(yi + 1, near), 1, 0))

        @pl.when(i == 3)
        def _():
            att_wait(att_half(yi + 2, near), 2, 0)
            att_wait(att_half(yi + 2, 1 - near), 2, 1)

        partial[y] = nt(weight[...], attended[y]).astype(BF16).reshape(NX, 2, WCOLS, TOK)
        remote(
            partial.at[y, :, 1 - core], paired.at[y], s_pp, r_pp.at[y], head=partner
        ).start()

    def pair_sum(i):
        y = lax.rem(yi + NY - turn(i), NY)
        remote(paired.at[y], paired.at[y], s_pp, r_pp.at[y], head=hd).wait_recv()
        for d in (2, 1, 3, 0):
            x = lax.rem(xi + d, NX)
            both = (
                partial[y, x, core].astype(F32) + paired[y, x].astype(F32)
            ).astype(BF16)
            if d:
                half_sum[y, x] = both
                remote(
                    half_sum.at[y, x],
                    arrived.at[y, xi],
                    s_part,
                    r_part.at[y],
                    head=x * 2 + core,
                ).start()
            else:
                arrived[y, xi] = both

    def plane_sum(i):
        y = lax.rem(yi + NY - turn(i), NY)
        remote(
            arrived.at[y, 0 : NX - 1],
            arrived.at[y, 0 : NX - 1],
            s_part,
            r_part.at[y],
            head=hd,
        ).wait_recv()
        total = arrived[y, 0].astype(F32)
        for x in range(1, NX):
            total = total + arrived[y, x].astype(F32)
        column_out[y] = total.astype(BF16)

        @pl.when(i > 0)
        def _():
            remote(
                column_out.at[y], column_in.at[yi], s_col, r_col, seq=zi * NY + y
            ).start()

        @pl.when(i == 0)
        def _():
            column_in[yi] = total.astype(BF16)

    def project_step(t, carry):
        pl.when(t < NY)(lambda: project(t))
        pl.when(t >= 1)(lambda: pair_sum(t - 1))
        return carry

    lax.fori_loop(0, NY + 1, project_step, 0)
    pl.loop(0, NY)(plane_sum)
    remote(
        column_in.at[0 : NY - 1], column_in.at[0 : NY - 1], s_col, r_col, seq=me
    ).wait_recv()
    for c in range(PART // HD):
        lanes = slice(c * HD, (c + 1) * HD)
        slab = column_in[...].astype(F32).reshape(PART, TOK)[c * HD : (c + 1) * HD, :]
        middle[:, lanes] = (res_ref[:, lanes].astype(F32) + jnp.transpose(slab)).astype(BF16)

    outgoing[...] = (
        nn(chosen_rows[...], middle[...]).astype(BF16).reshape(NSEQ, CAP, PART)
    )

    def my_rows(index):
        return pl.ds(pl.multiple_of(index * CAP, CAP), CAP)

    x_up = lax.rem(xi + 1, NX) * 2 + core
    x_down = lax.rem(xi + NX - 1, NX) * 2 + core
    x_far = lax.rem(xi + 2, NX) * 2 + core

    def half_rows(index, side):
        start = index * GROWS + side * (GROWS // 2)
        return pl.ds(pl.multiple_of(start, GROWS // 2), GROWS // 2)

    def group_rows(index):
        return pl.ds(pl.multiple_of(index * GROWS, GROWS), GROWS)

    @pl.loop(0, NSEQ - 1)
    def _(n):
        n = n + n // (NSEQ - GSRC)
        to = lax.rem(group + 1 + n // GSRC, NG) * GSRC + lax.rem(me + n, GSRC)
        remote(
            outgoing.at[to],
            rows_in.at[hd, my_rows(me)],
            s_disp,
            r_disp.at[group],
            seq=to,
        ).start()

    rows_in[hd, my_rows(me), :] = outgoing[me]

    def source_group(i):
        return lax.rem(group + NG - 1 - i, NG)

    def gather(i):
        g = source_group(i)
        part = group_rows(g)

        blocks = outgoing.at[0 : GSRC - 1 if i == NG - 1 else GSRC]
        remote(blocks, blocks, s_disp, r_disp.at[g], seq=me).wait_recv()
        block = rows_in.at[hd, part]
        remote(block, block, s_gath, r_gath.at[g, 0], head=x_up).start()
        remote(block, block, s_gath, r_gath.at[g, 1], head=x_down).start()
        remote(block, block, s_fwd, r_fwd.at[g], head=partner).start()

    def forward(i):
        g = source_group(i)
        part = group_rows(g)
        for side, source, to in ((0, x_down, x_up), (1, x_up, x_down)):
            block = rows_in.at[source, part]
            remote(block, block, s_gath, r_gath.at[g, side], head=hd).wait_recv()
            piece = rows_in.at[source, half_rows(g, side)]
            remote(piece, piece, s_gath, r_gath.at[g, 2 + side], head=to).start()
            remote(block, block, s_fwd, r_fwd.at[g], head=partner).start()

    def forward_far(i):
        g = source_group(i)
        for side in range(2):
            piece = rows_in.at[x_far, half_rows(g, side)]
            remote(piece, piece, s_gath, r_gath.at[g, 2 + side], head=hd).wait_recv()
        block = rows_in.at[x_far, group_rows(g)]
        remote(block, block, s_fwd, r_fwd.at[g], head=partner).start()

    def serve_up(pair):
        if pair == 0:
            for load in loads:
                load.wait()
        for n in range(2):
            g = source_group(2 * pair + n)
            part = group_rows(g)
            target = slice(n * GROWS, (n + 1) * GROWS)
            remote(
                rows_in.at[0:NX, 0:GROWS],
                rows_in.at[0:NX, 0:GROWS],
                s_fwd,
                r_fwd.at[g],
                head=hd,
            ).wait_recv()
            squares = jnp.zeros((GROWS, HD), F32)
            for h in range(NHEAD):
                block = rows_in[h, part, :].astype(F32)
                block = block * block
                for c in range(PART // HD):
                    squares = squares + block[:, c * HD : (c + 1) * HD]
            scale = lax.rsqrt(jnp.sum(squares, axis=1, keepdims=True) / D + EPSILON)
            for h in range(NHEAD):
                lanes = slice(h * PART, (h + 1) * PART)
                normed[target, lanes] = (
                    rows_in[h, part, :].astype(F32) * scale * ng_ref[:, lanes]
                ).astype(BF16)
        gated = nt(normed[...], gate[...])
        upped = nt(normed[...], up[...])
        hidden[...] = (gated / (1.0 + jnp.exp(-gated)) * upped).astype(BF16)

    def serve_down(pair):
        groups = [source_group(2 * pair + n) for n in range(2)]
        for h in range(NHEAD):
            lanes = slice(h * PART, (h + 1) * PART)
            product = nn(hidden[...], down[:, lanes]).astype(BF16)
            for n, g in enumerate(groups):
                result[h % 2, h // 2, group_rows(g), :] = product[
                    n * GROWS : (n + 1) * GROWS
                ]
        for g in groups:
            part = group_rows(g)
            remote(
                result.at[1 - core, :, part],
                pair_in.at[:, part],
                s_pair,
                r_pair.at[g],
                head=partner,
            ).start()

    def both_cores(x, rows):
        return result[core, x, rows, :].astype(F32) + pair_in[x, rows, :].astype(F32)

    def reduce_pair(i):
        g = source_group(i)
        part = group_rows(g)
        remote(
            pair_in.at[:, part], pair_in.at[:, part], s_pair, r_pair.at[g], head=hd
        ).wait_recv()
        far_sum[part, :] = both_cores(x_far // 2, part).astype(BF16)
        for side, to in ((0, x_up), (1, x_down)):
            piece = half_rows(g, side)
            remote(
                far_sum.at[piece],
                ring_in.at[piece],
                s_ring,
                r_ring.at[g, side],
                head=to,
            ).start()

    def reduce_mid(i):
        g = source_group(i)
        part = group_rows(g)
        for side, to in ((0, x_up), (1, x_down)):
            piece, other = half_rows(g, side), half_rows(g, 1 - side)
            near_sum[side, other, :] = both_cores(to // 2, other).astype(BF16)
            remote(
                ring_in.at[piece], ring_in.at[piece], s_ring, r_ring.at[g, side], head=hd
            ).wait_recv()
            near_sum[side, piece, :] = (
                both_cores(to // 2, piece) + ring_in[piece, :].astype(F32)
            ).astype(BF16)
            remote(
                near_sum.at[side, part],
                plane_in.at[side, part],
                s_plane,
                r_plane.at[g],
                head=to,
            ).start()

    def reduce_plane(i):
        g = source_group(i)
        part = group_rows(g)
        remote(
            plane_in.at[:, part], plane_in.at[:, part], s_plane, r_plane.at[g], head=hd
        ).wait_recv()
        total = both_cores(xi, part)
        for side in range(2):
            total = total + plane_in[side, part, :].astype(F32)
        summed[part, :] = total.astype(BF16)

        @pl.loop(0, GSRC)
        def _(j):
            to = g * GSRC + j

            @pl.when(to != me)
            def _():
                remote(
                    summed.at[my_rows(to)], returned.at[my_rows(me)], s_ret, r_ret, seq=to
                ).start()

    for stage, i in (
        (gather, 0),
        (gather, 1),
        (forward, 0),
        (gather, 2),
        (forward, 1),
        (gather, 3),
        (forward_far, 0),
        (forward_far, 1),
        (forward, 2),
        (serve_up, 0),
        (forward, 3),
        (serve_down, 0),
        (forward_far, 2),
        (reduce_pair, 0),
        (reduce_pair, 1),
        (forward_far, 3),
        (serve_up, 1),
        (reduce_mid, 0),
        (reduce_mid, 1),
        (serve_down, 1),
        (reduce_pair, 2),
        (reduce_plane, 0),
        (reduce_pair, 3),
        (reduce_plane, 1),
        (reduce_mid, 2),
        (reduce_mid, 3),
        (reduce_plane, 2),
        (reduce_plane, 3),
    ):
        stage(i)
    returned[my_rows(me), :] = summed[my_rows(me), :]

    slots = (NSEQ - 1) * CAP
    remote(
        returned.at[0:slots], returned.at[0:slots], s_ret, r_ret, seq=me
    ).wait_recv()
    for c in range(PART // HD):
        lanes = slice(c * HD, (c + 1) * HD)
        out_ref[:, lanes] = (
            middle[:, lanes].astype(F32)
            + (
                nn(picks[0], returned[:, lanes]) * mixes[0]
                + nn(picks[1], returned[:, lanes]) * mixes[1]
            )
        ).astype(BF16)

    remote(
        outgoing.at[0 : NSEQ - 1], outgoing.at[0 : NSEQ - 1], s_disp, r_disp.at[0], seq=me
    ).wait_send()
    remote(
        rows_in.at[0 : NX - 1], rows_in.at[0 : NX - 1], s_gath, r_gath.at[0, 0], head=hd
    ).wait_send()
    remote(rows_in.at[0:NX], rows_in.at[0:NX], s_fwd, r_fwd.at[0], head=hd).wait_send()
    remote(pair_in, pair_in, s_pair, r_pair.at[0], head=hd).wait_send()
    remote(far_sum, far_sum, s_ring, r_ring.at[0, 0], head=hd).wait_send()
    remote(plane_in, plane_in, s_plane, r_plane.at[0], head=hd).wait_send()
    remote(
        returned.at[0:slots], returned.at[0:slots], s_ret, r_ret, seq=me
    ).wait_send()
    remote(
        own_state.at[0:others], all_state.at[0:others], s_state, r_state, seq=me
    ).wait_send()
    remote(
        all_info.at[0:others], all_info.at[0:others], s_info, r_info, seq=me
    ).wait_send()
    remote(
        own_carry.at[0:others], all_carry.at[0:others], s_carry, r_carry.at[0], seq=me
    ).wait_send()
    remote(attended.at[0:3], attended.at[0:3], s_att, r_att.at[0, 0], seq=me).wait_send()
    w_copy(pl.ds(0, (NZ - 1) * WCOLS), 0, me, 0).wait_send()
    remote(paired, paired, s_pp, r_pp.at[0], head=hd).wait_send()
    remote(
        arrived.at[:, 0 : NX - 1],
        arrived.at[:, 0 : NX - 1],
        s_part,
        r_part.at[0],
        head=hd,
    ).wait_send()
    remote(
        column_in.at[0 : NY - 1], column_in.at[0 : NY - 1], s_col, r_col, seq=me
    ).wait_send()


def layer(*operands):
    vmem = pl.BlockSpec(memory_space=pltpu.VMEM)
    anywhere = pl.BlockSpec(memory_space=pl.ANY)
    dma = pltpu.SemaphoreType.DMA
    return pl.pallas_call(
        layer_kernel,
        out_shape=jax.ShapeDtypeStruct((TOK, PART), BF16),
        in_specs=[anywhere] * 14,
        out_specs=vmem,
        scratch_shapes=[
            pltpu.VMEM((TOK, HEADS * HD), BF16),
            pltpu.VMEM((TOK, HEADS * HD), BF16),
            pltpu.VMEM((TOK, HEADS * HD), BF16),
            pltpu.VMEM((HEADS, TOK), F32),
            pltpu.VMEM((1, TOK), jnp.int32),
            pltpu.VMEM((1, HEADS * HD), F32),
            pltpu.VMEM((TOK, PART), BF16),
            pltpu.VMEM((2, TOK), jnp.int32),
            pltpu.VMEM((2, TOK), F32),
            pltpu.VMEM((1, D), F32),
            pltpu.VMEM((HEADS, TOK), F32),
            pltpu.VMEM((HEADS, TOK), F32),
            pltpu.VMEM((NSEQ, 32, HD), BF16),
            pltpu.VMEM((HEADS, 1, TOK), F32),
            pltpu.VMEM((NSEQ, 32, HD), BF16),
            pltpu.VMEM((NSEQ, 1, TOK), F32),
            pltpu.VMEM((NSEQ, 32, HD), BF16),
            pltpu.VMEM((NSEQ, 32, HD), BF16),
            pltpu.VMEM((TOK, HEADS * HD), F32),
            pltpu.VMEM((NY, TOK, HEADS * HD), BF16),
            pltpu.VMEM((NZ * WCOLS, HEADS * HD), BF16),
            pltpu.VMEM((NY, NX, 2, WCOLS, TOK), BF16),
            pltpu.VMEM((NY, NX, WCOLS, TOK), BF16),
            pltpu.VMEM((NY, NX, WCOLS, TOK), BF16),
            pltpu.VMEM((NY, NX, WCOLS, TOK), BF16),
            pltpu.VMEM((NY, WCOLS, TOK), BF16),
            pltpu.VMEM((NY, WCOLS, TOK), BF16),
            pltpu.VMEM((TOK, PART), BF16),
            pltpu.VMEM((SLOTS, TOK), BF16),
            pltpu.VMEM((2, TOK, SLOTS), BF16),
            pltpu.VMEM((2, TOK, TOK), F32),
            pltpu.VMEM((FF, D), BF16),
            pltpu.VMEM((FF, D), BF16),
            pltpu.VMEM((FF, D), BF16),
            pltpu.VMEM((NSEQ, CAP, PART), BF16),
            pltpu.VMEM((NHEAD, SLOTS, PART), BF16),
            pltpu.VMEM((2 * GROWS, D), BF16),
            pltpu.VMEM((2 * GROWS, FF), BF16),
            pltpu.VMEM((2, NX, SLOTS, PART), BF16),
            pltpu.VMEM((NX, SLOTS, PART), BF16),
            pltpu.VMEM((SLOTS, PART), BF16),
            pltpu.VMEM((SLOTS, PART), BF16),
            pltpu.VMEM((2, SLOTS, PART), BF16),
            pltpu.VMEM((2, SLOTS, PART), BF16),
            pltpu.VMEM((SLOTS, PART), BF16),
            pltpu.VMEM((SLOTS, PART), BF16),
            dma,
            dma,
            dma,
            dma,
            dma,
            dma((2,)),
            dma,
            dma((3, 2)),
            dma,
            dma((2, 4)),
            dma,
            dma((NY,)),
            dma,
            dma((NY,)),
            dma,
            dma,
            dma((3,)),
            dma((11,)),
            dma,
            dma((NG,)),
            dma,
            dma((NG, 4)),
            dma,
            dma((NG,)),
            dma,
            dma((NG,)),
            dma,
            dma((NG, 2)),
            dma,
            dma((NG,)),
            dma,
            dma,
        ],
        compiler_params=pltpu.CompilerParams(
            collective_id=0, has_side_effects=True, vmem_limit_bytes=VMEM_LIMIT
        ),
        name="layer",
    )(*operands)


def shards(
    queries,
    key_vectors,
    value_vectors,
    log_decay,
    doc_ids,
    head_gain,
    output_weight,
    residual,
    norm_gain,
    routing,
    route_weights,
    gate_weight,
    up_weight,
    down_weight,
):
    return layer(
        queries,
        key_vectors,
        value_vectors,
        log_decay.T,
        doc_ids.reshape(1, -1),
        head_gain.reshape(1, -1),
        output_weight.T,
        residual,
        routing.T,
        route_weights.T,
        norm_gain.reshape(1, -1),
        gate_weight[0].T,
        up_weight[0].T,
        down_weight[0],
    )


def solution(mesh):
    in_specs = (
        P("seq", "head"),
        P("seq", "head"),
        P("seq", "head"),
        P("seq", "head"),
        P("seq"),
        P("head"),
        P("head", "seq"),
        P("seq", "head"),
        P(),
        P("seq", None),
        P("seq", None),
        P("seq", None, "head"),
        P("seq", None, "head"),
        P("seq", "head", None),
    )
    return jax.shard_map(
        shards, mesh=mesh, in_specs=in_specs, out_specs=P("seq", "head"), check_vma=False
    )
```

```python
import functools

import jax
import jax.numpy as jnp
from jax import lax
from jax.experimental import pallas as pl
from jax.experimental.pallas import tpu as pltpu
from jax.sharding import PartitionSpec as P

MESH = pl.DeviceIdType.MESH
F32, BF16 = jnp.float32, jnp.bfloat16
EPSILON = 1e-06
NZ, NY, NX = 8, 4, 4
NSEQ, NHEAD = NZ * NY, 2 * NX
TOK, HEADS, HD = 128, 8, 128
WCOLS = 96
PART = 384
D = PART * NHEAD
CAP = 16
NG = 4
GSRC = NSEQ // NG
GROWS = GSRC * CAP
SLOTS = NSEQ * CAP
FF = 576
VMEM_LIMIT = 60 * 1024 * 1024


def nt(a, b):
    return lax.dot_general(a, b, (((1,), (1,)), ((), ())), preferred_element_type=F32)


def nn(a, b):
    return jnp.dot(a, b, preferred_element_type=F32)


def remote(src, dst, send_sem, recv_sem, **device):
    return pltpu.make_async_remote_copy(
        src_ref=src,
        dst_ref=dst,
        send_sem=send_sem,
        recv_sem=recv_sem,
        device_id=device,
        device_id_type=MESH,
    )


def greet(me, hd):
    barrier = pltpu.get_barrier_semaphore()

    @pl.loop(1, NSEQ)
    def _(d):
        pl.semaphore_signal(
            barrier, inc=1, device_id={"seq": lax.rem(me + d, NSEQ)}, device_id_type=MESH
        )

    @pl.loop(1, NHEAD)
    def _(d):
        pl.semaphore_signal(
            barrier, inc=1, device_id={"head": lax.rem(hd + d, NHEAD)}, device_id_type=MESH
        )

    return barrier


def turn(i):
    return i + i // 2 - 2 * (i // 3)


def columns(row):
    return jnp.transpose(jnp.broadcast_to(row, (TOK, TOK)))


def layer_kernel(
    q_hbm,
    k_hbm,
    v_hbm,
    ld_hbm,
    doc_hbm,
    hg_hbm,
    w_hbm,
    res_hbm,
    rout_hbm,
    mix_hbm,
    ng_hbm,
    gate_hbm,
    up_hbm,
    down_hbm,
    out_ref,
    q_ref,
    k_ref,
    v_ref,
    ld_ref,
    doc_ref,
    hg_ref,
    res_ref,
    rout_ref,
    mix_ref,
    ng_ref,
    decay,
    reaches,
    own_state,
    own_info,
    all_state,
    all_info,
    own_carry,
    all_carry,
    inner,
    attended,
    weight,
    partial,
    paired,
    half_sum,
    arrived,
    column_out,
    column_in,
    middle,
    chosen_rows,
    picks,
    mixes,
    gate,
    up,
    down,
    outgoing,
    rows_in,
    normed,
    hidden,
    result,
    pair_in,
    far_sum,
    ring_in,
    near_sum,
    plane_in,
    summed,
    returned,
    s_state,
    r_state,
    s_info,
    r_info,
    s_carry,
    r_carry,
    s_att,
    r_att,
    s_w,
    r_w,
    s_pp,
    r_pp,
    s_part,
    r_part,
    s_col,
    r_col,
    s_load,
    s_in,
    s_disp,
    r_disp,
    s_gath,
    r_gath,
    s_fwd,
    r_fwd,
    s_pair,
    r_pair,
    s_ring,
    r_ring,
    s_plane,
    r_plane,
    s_ret,
    r_ret,
):
    me, hd = lax.axis_index("seq"), lax.axis_index("head")
    zi, yi = me // NY, lax.rem(me, NY)
    xi, core = hd // 2, lax.rem(hd, 2)
    partner = xi * 2 + 1 - core
    group = me // GSRC
    barrier = greet(me, hd)
    loads = [
        pltpu.make_async_copy(gate_hbm, gate, s_load.at[0]),
        pltpu.make_async_copy(up_hbm, up, s_load.at[1]),
        pltpu.make_async_copy(down_hbm, down, s_load.at[2]),
    ]

    def w_rows(z, start=0, size=WCOLS):
        return pl.ds(pl.multiple_of(lax.rem(z + NZ, NZ) * WCOLS + start, 16), size)

    fetches = [
        pltpu.make_async_copy(source, target, s_in.at[n])
        for n, (source, target) in enumerate(
            (
                (ld_hbm, ld_ref),
                (doc_hbm, doc_ref),
                (k_hbm, k_ref),
                (v_hbm, v_ref),
                (w_hbm, weight.at[w_rows(zi)]),
                (q_hbm, q_ref),
                (rout_hbm, rout_ref),
                (mix_hbm, mix_ref),
                (hg_hbm, hg_ref),
                (res_hbm, res_ref),
                (ng_hbm, ng_ref),
            )
        )
    ]
    for fetch in fetches:
        fetch.start()
    for load in loads:
        load.start()
    for fetch in fetches[0:4]:
        fetch.wait()

    rows = lax.broadcasted_iota(jnp.int32, (TOK, TOK), 0)
    cols = lax.broadcasted_iota(jnp.int32, (TOK, TOK), 1)
    upper = (rows <= cols).astype(F32)
    sums = jnp.dot(
        ld_ref[...], upper, preferred_element_type=F32, precision=lax.Precision.HIGHEST
    )
    decay[...] = sums
    last = sums[:, TOK - 1 : TOK]
    doc = doc_ref[...].astype(F32)
    doc_first, doc_last = doc[:, 0:1], doc[:, TOK - 1 : TOK]
    tail = jnp.exp(last - sums) * (doc == doc_last).astype(F32)
    gain = jnp.exp(last) * (doc_first == doc_last).astype(F32)
    lane = lax.broadcasted_iota(jnp.int32, (HEADS, TOK), 1)
    info = jnp.where(lane < 32, gain, jnp.where(lane < 64, doc_first, doc_last))
    for h in range(HEADS):
        own_info[h] = info[h : h + 1, :]
    for h in range(HEADS):
        lanes = slice(h * HD, (h + 1) * HD)
        key_t = jnp.transpose(k_ref[:, lanes].astype(F32))
        state = nn((key_t * tail[h : h + 1, :]).astype(BF16), v_ref[:, lanes])
        own_state[4 * h : 4 * h + 4] = state.astype(BF16).reshape(4, 32, HD)

    pl.semaphore_wait(barrier, NSEQ + NHEAD - 2)

    @pl.loop(1, NSEQ)
    def _(n):
        to = lax.rem(me + n, NSEQ)
        remote(own_info.at[to // 4], all_info.at[me], s_info, r_info, seq=to).start()
        remote(own_state.at[to], all_state.at[me], s_state, r_state, seq=to).start()

    all_state[me] = own_state[me]
    all_info[me] = own_info[me // 4]

    right = lax.rem(zi + 1, NZ) * NY + yi
    left = lax.rem(zi + NZ - 1, NZ) * NY + yi
    half = WCOLS // 2

    def w_copy(rows, k, to, side):
        block = weight.at[rows]
        return remote(block, block, s_w, r_w.at[side, k], seq=to)

    def w_step(k):
        w_copy(w_rows(zi - 1 - k), k, me, 0).wait_recv()
        from_left = w_rows(zi - 1 - k) if k < 2 else w_rows(zi - 1 - k, 0, half)
        w_copy(from_left, k + 1, right, 0).start()
        w_copy(w_rows(zi + 1 + k), k, me, 1).wait_recv()
        from_right = w_rows(zi + 1 + k) if k < 2 else w_rows(zi + 1 + k, half, half)
        w_copy(from_right, k + 1, left, 1).start()

    fetches[4].wait()
    w_copy(w_rows(zi), 0, right, 0).start()
    w_copy(w_rows(zi), 0, left, 1).start()
    for fetch in fetches[5:]:
        fetch.wait()

    doc_rows = jnp.broadcast_to(doc, (TOK, TOK))
    kept = (cols <= rows) & (jnp.transpose(doc_rows) == doc_rows)
    for h in range(HEADS):
        lanes = slice(h * HD, (h + 1) * HD)
        decay_row = jnp.broadcast_to(decay[h : h + 1, :], (TOK, TOK))
        gap = jnp.transpose(decay_row) - decay_row
        factor = jnp.where(kept, jnp.exp(jnp.minimum(gap, 0.0)), 0.0)
        weighted = (nt(q_ref[:, lanes], k_ref[:, lanes]) * factor).astype(BF16)
        inner[:, lanes] = nn(weighted, v_ref[:, lanes])
    expert = lax.broadcasted_iota(jnp.int32, (NSEQ, TOK), 0)
    hits = [(expert == rout_ref[j : j + 1, :]).astype(F32) for j in range(2)]
    earlier = (
        lax.broadcasted_iota(jnp.int32, (TOK, TOK), 0)
        < lax.broadcasted_iota(jnp.int32, (TOK, TOK), 1)
    ).astype(BF16)
    count = nn((hits[0] + hits[1]).astype(BF16), earlier)
    places = [
        rout_ref[j : j + 1, :].astype(F32) * CAP
        + jnp.sum(hits[j] * count, axis=0, keepdims=True)
        for j in range(2)
    ]
    slot = lax.broadcasted_iota(jnp.int32, (NSEQ * CAP, TOK), 0).astype(F32)
    chosen = (slot == places[0]).astype(F32) + (slot == places[1]).astype(F32)
    chosen_rows[...] = chosen.astype(BF16)
    lane = lax.broadcasted_iota(jnp.int32, (TOK, NSEQ * CAP), 1).astype(F32)
    for j in range(2):
        picks[j] = (lane == columns(places[j])[:, 0:1]).astype(BF16)
        mixes[j] = columns(mix_ref[j : j + 1, :])


    others = NSEQ - 1
    remote(
        own_state.at[0:others], all_state.at[0:others], s_state, r_state, seq=me
    ).wait_recv()
    remote(
        all_info.at[0:others], all_info.at[0:others], s_info, r_info, seq=me
    ).wait_recv()

    carried, before = jnp.zeros((32, HD), F32), jnp.full((1, 1), -1.0, F32)
    for b in range(NSEQ):
        own_carry[b] = carried.astype(BF16)
        row = all_info[b]
        through = jnp.where(row[:, 32:33] == before, row[:, 0:1], 0.0)
        carried, before = all_state[b].astype(F32) + through * carried, row[:, 64:65]

    @pl.loop(1, NSEQ)
    def _(n):
        to = lax.rem(me + n, NSEQ)
        remote(
            own_carry.at[to], all_carry.at[me], s_carry, r_carry.at[me // 16], seq=to
        ).start()

    all_carry[me] = own_carry[me]
    before_doc = all_info[jnp.maximum(me - 1, 0)][:, 64:65]
    before_doc = jnp.where(jnp.full((1, 1), me, jnp.int32) == 0, -1.0, before_doc)
    w_step(0)
    reaches[...] = jnp.exp(decay[...]) * (doc == before_doc).astype(F32)
    y_up = zi * NY + lax.rem(yi + 1, NY)
    y_down = zi * NY + lax.rem(yi + NY - 1, NY)
    near = me // 16

    def half_lanes(part):
        return pl.ds(pl.multiple_of(part * 512, 512), 512)

    def att_half(y, part):
        return attended.at[lax.rem(y + NY, NY), :, half_lanes(part)]

    def att_wait(block, side, part):
        remote(block, block, s_att, r_att.at[side, part], seq=me).wait_recv()

    for order in range(2):
        part = near if order == 0 else 1 - near
        slabs = own_carry.at[0 : 15 if order == 0 else 16]
        remote(slabs, slabs, s_carry, r_carry.at[part], seq=me).wait_recv()
        for j in range(4):
            h = part * 4 + j
            lanes = pl.ds(pl.multiple_of(h * HD, HD), HD)
            carried = all_carry[pl.ds(4 * h, 4)].reshape(HD, HD)
            raw = inner[:, lanes] + nn(q_ref[:, lanes], carried) * columns(
                reaches[pl.ds(h, 1), :]
            )
            scale = lax.rsqrt(jnp.mean(raw * raw, axis=1, keepdims=True) + EPSILON)
            attended[yi, :, lanes] = (raw * scale * hg_ref[:, lanes]).astype(BF16)
            if j % 2 == 1:
                pair = pl.ds(pl.multiple_of((h - 1) * HD, 2 * HD), 2 * HD)
                block = attended.at[yi, :, pair]
                remote(block, block, s_att, r_att.at[0, order], seq=y_up).start()
                remote(block, block, s_att, r_att.at[1, order], seq=y_down).start()
        if order == 0:
            w_step(1)

    block = att_half(yi - 1, near)
    att_wait(block, 0, 0)
    remote(block, block, s_att, r_att.at[2, 0], seq=y_up).start()
    w_step(2)
    block = att_half(yi + 1, 1 - near)
    att_wait(block, 1, 1)
    remote(block, block, s_att, r_att.at[2, 1], seq=y_down).start()
    w_copy(w_rows(zi + 4, 0, half), 3, me, 0).wait_recv()
    w_copy(w_rows(zi + 4, half, half), 3, me, 1).wait_recv()

    def project(i):
        y = lax.rem(yi + NY - turn(i), NY)
        pl.when(i == 1)(lambda: att_wait(att_half(yi - 1, 1 - near), 0, 1))
        pl.when(i == 2)(lambda: att_wait(att_half(yi + 1, near), 1, 0))

        @pl.when(i == 3)
        def _():
            att_wait(att_half(yi + 2, near), 2, 0)
            att_wait(att_half(yi + 2, 1 - near), 2, 1)

        partial[y] = nt(weight[...], attended[y]).astype(BF16).reshape(NX, 2, WCOLS, TOK)
        remote(
            partial.at[y, :, 1 - core], paired.at[y], s_pp, r_pp.at[y], head=partner
        ).start()

    def pair_sum(i):
        y = lax.rem(yi + NY - turn(i), NY)
        remote(paired.at[y], paired.at[y], s_pp, r_pp.at[y], head=hd).wait_recv()
        for d in (2, 1, 3, 0):
            x = lax.rem(xi + d, NX)
            both = (
                partial[y, x, core].astype(F32) + paired[y, x].astype(F32)
            ).astype(BF16)
            if d:
                half_sum[y, x] = both
                remote(
                    half_sum.at[y, x],
                    arrived.at[y, xi],
                    s_part,
                    r_part.at[y],
                    head=x * 2 + core,
                ).start()
            else:
                arrived[y, xi] = both

    def plane_sum(i):
        y = lax.rem(yi + NY - turn(i), NY)
        remote(
            arrived.at[y, 0 : NX - 1],
            arrived.at[y, 0 : NX - 1],
            s_part,
            r_part.at[y],
            head=hd,
        ).wait_recv()
        total = arrived[y, 0].astype(F32)
        for x in range(1, NX):
            total = total + arrived[y, x].astype(F32)
        column_out[y] = total.astype(BF16)

        @pl.when(i > 0)
        def _():
            remote(
                column_out.at[y], column_in.at[yi], s_col, r_col, seq=zi * NY + y
            ).start()

        @pl.when(i == 0)
        def _():
            column_in[yi] = total.astype(BF16)

    def project_step(t, carry):
        pl.when(t < NY)(lambda: project(t))
        pl.when(t >= 1)(lambda: pair_sum(t - 1))
        return carry

    lax.fori_loop(0, NY + 1, project_step, 0)
    pl.loop(0, NY)(plane_sum)
    remote(
        column_in.at[0 : NY - 1], column_in.at[0 : NY - 1], s_col, r_col, seq=me
    ).wait_recv()
    for c in range(PART // HD):
        lanes = slice(c * HD, (c + 1) * HD)
        slab = column_in[...].astype(F32).reshape(PART, TOK)[c * HD : (c + 1) * HD, :]
        middle[:, lanes] = (res_ref[:, lanes].astype(F32) + jnp.transpose(slab)).astype(BF16)

    outgoing[...] = (
        nn(chosen_rows[...], middle[...]).astype(BF16).reshape(NSEQ, CAP, PART)
    )

    def my_rows(index):
        return pl.ds(pl.multiple_of(index * CAP, CAP), CAP)

    x_up = lax.rem(xi + 1, NX) * 2 + core
    x_down = lax.rem(xi + NX - 1, NX) * 2 + core
    x_far = lax.rem(xi + 2, NX) * 2 + core

    def half_rows(index, side):
        start = index * GROWS + side * (GROWS // 2)
        return pl.ds(pl.multiple_of(start, GROWS // 2), GROWS // 2)

    def group_rows(index):
        return pl.ds(pl.multiple_of(index * GROWS, GROWS), GROWS)

    @pl.loop(0, NSEQ - 1)
    def _(n):
        n = n + n // (NSEQ - GSRC)
        to = lax.rem(group + 1 + n // GSRC, NG) * GSRC + lax.rem(me + n, GSRC)
        remote(
            outgoing.at[to],
            rows_in.at[hd, my_rows(me)],
            s_disp,
            r_disp.at[group],
            seq=to,
        ).start()

    rows_in[hd, my_rows(me), :] = outgoing[me]

    def source_group(i):
        return lax.rem(group + NG - 1 - i, NG)

    def gather(i):
        g = source_group(i)
        part = group_rows(g)

        blocks = outgoing.at[0 : GSRC - 1 if i == NG - 1 else GSRC]
        remote(blocks, blocks, s_disp, r_disp.at[g], seq=me).wait_recv()
        block = rows_in.at[hd, part]
        remote(block, block, s_gath, r_gath.at[g, 0], head=x_up).start()
        remote(block, block, s_gath, r_gath.at[g, 1], head=x_down).start()
        remote(block, block, s_fwd, r_fwd.at[g], head=partner).start()

    def forward(i):
        g = source_group(i)
        part = group_rows(g)
        for side, source, to in ((0, x_down, x_up), (1, x_up, x_down)):
            block = rows_in.at[source, part]
            remote(block, block, s_gath, r_gath.at[g, side], head=hd).wait_recv()
            piece = rows_in.at[source, half_rows(g, side)]
            remote(piece, piece, s_gath, r_gath.at[g, 2 + side], head=to).start()
            remote(block, block, s_fwd, r_fwd.at[g], head=partner).start()

    def forward_far(i):
        g = source_group(i)
        for side in range(2):
            piece = rows_in.at[x_far, half_rows(g, side)]
            remote(piece, piece, s_gath, r_gath.at[g, 2 + side], head=hd).wait_recv()
        block = rows_in.at[x_far, group_rows(g)]
        remote(block, block, s_fwd, r_fwd.at[g], head=partner).start()

    def serve_up(pair):
        if pair == 0:
            for load in loads:
                load.wait()
        for n in range(2):
            g = source_group(2 * pair + n)
            part = group_rows(g)
            target = slice(n * GROWS, (n + 1) * GROWS)
            remote(
                rows_in.at[0:NX, 0:GROWS],
                rows_in.at[0:NX, 0:GROWS],
                s_fwd,
                r_fwd.at[g],
                head=hd,
            ).wait_recv()
            squares = jnp.zeros((GROWS, HD), F32)
            for h in range(NHEAD):
                block = rows_in[h, part, :].astype(F32)
                block = block * block
                for c in range(PART // HD):
                    squares = squares + block[:, c * HD : (c + 1) * HD]
            scale = lax.rsqrt(jnp.sum(squares, axis=1, keepdims=True) / D + EPSILON)
            for h in range(NHEAD):
                lanes = slice(h * PART, (h + 1) * PART)
                normed[target, lanes] = (
                    rows_in[h, part, :].astype(F32) * scale * ng_ref[:, lanes]
                ).astype(BF16)
        gated = nt(normed[...], gate[...])
        upped = nt(normed[...], up[...])
        hidden[...] = (gated / (1.0 + jnp.exp(-gated)) * upped).astype(BF16)

    def serve_down(pair):
        groups = [source_group(2 * pair + n) for n in range(2)]
        for h in range(NHEAD):
            lanes = slice(h * PART, (h + 1) * PART)
            product = nn(hidden[...], down[:, lanes]).astype(BF16)
            for n, g in enumerate(groups):
                result[h % 2, h // 2, group_rows(g), :] = product[
                    n * GROWS : (n + 1) * GROWS
                ]
        for g in groups:
            part = group_rows(g)
            remote(
                result.at[1 - core, :, part],
                pair_in.at[:, part],
                s_pair,
                r_pair.at[g],
                head=partner,
            ).start()

    def both_cores(x, rows):
        return result[core, x, rows, :].astype(F32) + pair_in[x, rows, :].astype(F32)

    def reduce_pair(i):
        g = source_group(i)
        part = group_rows(g)
        remote(
            pair_in.at[:, part], pair_in.at[:, part], s_pair, r_pair.at[g], head=hd
        ).wait_recv()
        far_sum[part, :] = both_cores(x_far // 2, part).astype(BF16)
        for side, to in ((0, x_up), (1, x_down)):
            piece = half_rows(g, side)
            remote(
                far_sum.at[piece],
                ring_in.at[piece],
                s_ring,
                r_ring.at[g, side],
                head=to,
            ).start()

    def reduce_mid(i):
        g = source_group(i)
        part = group_rows(g)
        for side, to in ((0, x_up), (1, x_down)):
            piece, other = half_rows(g, side), half_rows(g, 1 - side)
            near_sum[side, other, :] = both_cores(to // 2, other).astype(BF16)
            remote(
                ring_in.at[piece], ring_in.at[piece], s_ring, r_ring.at[g, side], head=hd
            ).wait_recv()
            near_sum[side, piece, :] = (
                both_cores(to // 2, piece) + ring_in[piece, :].astype(F32)
            ).astype(BF16)
            remote(
                near_sum.at[side, part],
                plane_in.at[side, part],
                s_plane,
                r_plane.at[g],
                head=to,
            ).start()

    def reduce_plane(i):
        g = source_group(i)
        part = group_rows(g)
        remote(
            plane_in.at[:, part], plane_in.at[:, part], s_plane, r_plane.at[g], head=hd
        ).wait_recv()
        total = both_cores(xi, part)
        for side in range(2):
            total = total + plane_in[side, part, :].astype(F32)
        summed[part, :] = total.astype(BF16)

        @pl.loop(0, GSRC)
        def _(j):
            to = g * GSRC + j

            @pl.when(to != me)
            def _():
                remote(
                    summed.at[my_rows(to)], returned.at[my_rows(me)], s_ret, r_ret, seq=to
                ).start()

    for stage, i in (
        (gather, 0),
        (gather, 1),
        (forward, 0),
        (gather, 2),
        (forward, 1),
        (gather, 3),
        (forward_far, 0),
        (forward_far, 1),
        (forward, 2),
        (serve_up, 0),
        (forward, 3),
        (serve_down, 0),
        (forward_far, 2),
        (reduce_pair, 0),
        (reduce_pair, 1),
        (forward_far, 3),
        (serve_up, 1),
        (reduce_mid, 0),
        (reduce_mid, 1),
        (serve_down, 1),
        (reduce_pair, 2),
        (reduce_pair, 3),
        (reduce_plane, 0),
        (reduce_plane, 1),
        (reduce_mid, 2),
        (reduce_mid, 3),
        (reduce_plane, 2),
        (reduce_plane, 3),
    ):
        stage(i)
    returned[my_rows(me), :] = summed[my_rows(me), :]

    slots = (NSEQ - 1) * CAP
    remote(
        returned.at[0:slots], returned.at[0:slots], s_ret, r_ret, seq=me
    ).wait_recv()
    for c in range(PART // HD):
        lanes = slice(c * HD, (c + 1) * HD)
        out_ref[:, lanes] = (
            middle[:, lanes].astype(F32)
            + (
                nn(picks[0], returned[:, lanes]) * mixes[0]
                + nn(picks[1], returned[:, lanes]) * mixes[1]
            )
        ).astype(BF16)

    remote(
        outgoing.at[0 : NSEQ - 1], outgoing.at[0 : NSEQ - 1], s_disp, r_disp.at[0], seq=me
    ).wait_send()
    remote(
        rows_in.at[0 : NX - 1], rows_in.at[0 : NX - 1], s_gath, r_gath.at[0, 0], head=hd
    ).wait_send()
    remote(rows_in.at[0:NX], rows_in.at[0:NX], s_fwd, r_fwd.at[0], head=hd).wait_send()
    remote(pair_in, pair_in, s_pair, r_pair.at[0], head=hd).wait_send()
    remote(far_sum, far_sum, s_ring, r_ring.at[0, 0], head=hd).wait_send()
    remote(plane_in, plane_in, s_plane, r_plane.at[0], head=hd).wait_send()
    remote(
        returned.at[0:slots], returned.at[0:slots], s_ret, r_ret, seq=me
    ).wait_send()
    remote(
        own_state.at[0:others], all_state.at[0:others], s_state, r_state, seq=me
    ).wait_send()
    remote(
        all_info.at[0:others], all_info.at[0:others], s_info, r_info, seq=me
    ).wait_send()
    remote(
        own_carry.at[0:others], all_carry.at[0:others], s_carry, r_carry.at[0], seq=me
    ).wait_send()
    remote(attended.at[0:3], attended.at[0:3], s_att, r_att.at[0, 0], seq=me).wait_send()
    w_copy(pl.ds(0, (NZ - 1) * WCOLS), 0, me, 0).wait_send()
    remote(paired, paired, s_pp, r_pp.at[0], head=hd).wait_send()
    remote(
        arrived.at[:, 0 : NX - 1],
        arrived.at[:, 0 : NX - 1],
        s_part,
        r_part.at[0],
        head=hd,
    ).wait_send()
    remote(
        column_in.at[0 : NY - 1], column_in.at[0 : NY - 1], s_col, r_col, seq=me
    ).wait_send()


def layer(*operands):
    vmem = pl.BlockSpec(memory_space=pltpu.VMEM)
    anywhere = pl.BlockSpec(memory_space=pl.ANY)
    dma = pltpu.SemaphoreType.DMA
    return pl.pallas_call(
        layer_kernel,
        out_shape=jax.ShapeDtypeStruct((TOK, PART), BF16),
        in_specs=[anywhere] * 14,
        out_specs=vmem,
        scratch_shapes=[
            pltpu.VMEM((TOK, HEADS * HD), BF16),
            pltpu.VMEM((TOK, HEADS * HD), BF16),
            pltpu.VMEM((TOK, HEADS * HD), BF16),
            pltpu.VMEM((HEADS, TOK), F32),
            pltpu.VMEM((1, TOK), jnp.int32),
            pltpu.VMEM((1, HEADS * HD), F32),
            pltpu.VMEM((TOK, PART), BF16),
            pltpu.VMEM((2, TOK), jnp.int32),
            pltpu.VMEM((2, TOK), F32),
            pltpu.VMEM((1, D), F32),
            pltpu.VMEM((HEADS, TOK), F32),
            pltpu.VMEM((HEADS, TOK), F32),
            pltpu.VMEM((NSEQ, 32, HD), BF16),
            pltpu.VMEM((HEADS, 1, TOK), F32),
            pltpu.VMEM((NSEQ, 32, HD), BF16),
            pltpu.VMEM((NSEQ, 1, TOK), F32),
            pltpu.VMEM((NSEQ, 32, HD), BF16),
            pltpu.VMEM((NSEQ, 32, HD), BF16),
            pltpu.VMEM((TOK, HEADS * HD), F32),
            pltpu.VMEM((NY, TOK, HEADS * HD), BF16),
            pltpu.VMEM((NZ * WCOLS, HEADS * HD), BF16),
            pltpu.VMEM((NY, NX, 2, WCOLS, TOK), BF16),
            pltpu.VMEM((NY, NX, WCOLS, TOK), BF16),
            pltpu.VMEM((NY, NX, WCOLS, TOK), BF16),
            pltpu.VMEM((NY, NX, WCOLS, TOK), BF16),
            pltpu.VMEM((NY, WCOLS, TOK), BF16),
            pltpu.VMEM((NY, WCOLS, TOK), BF16),
            pltpu.VMEM((TOK, PART), BF16),
            pltpu.VMEM((SLOTS, TOK), BF16),
            pltpu.VMEM((2, TOK, SLOTS), BF16),
            pltpu.VMEM((2, TOK, TOK), F32),
            pltpu.VMEM((FF, D), BF16),
            pltpu.VMEM((FF, D), BF16),
            pltpu.VMEM((FF, D), BF16),
            pltpu.VMEM((NSEQ, CAP, PART), BF16),
            pltpu.VMEM((NHEAD, SLOTS, PART), BF16),
            pltpu.VMEM((2 * GROWS, D), BF16),
            pltpu.VMEM((2 * GROWS, FF), BF16),
            pltpu.VMEM((2, NX, SLOTS, PART), BF16),
            pltpu.VMEM((NX, SLOTS, PART), BF16),
            pltpu.VMEM((SLOTS, PART), BF16),
            pltpu.VMEM((SLOTS, PART), BF16),
            pltpu.VMEM((2, SLOTS, PART), BF16),
            pltpu.VMEM((2, SLOTS, PART), BF16),
            pltpu.VMEM((SLOTS, PART), BF16),
            pltpu.VMEM((SLOTS, PART), BF16),
            dma,
            dma,
            dma,
            dma,
            dma,
            dma((2,)),
            dma,
            dma((3, 2)),
            dma,
            dma((2, 4)),
            dma,
            dma((NY,)),
            dma,
            dma((NY,)),
            dma,
            dma,
            dma((3,)),
            dma((11,)),
            dma,
            dma((NG,)),
            dma,
            dma((NG, 4)),
            dma,
            dma((NG,)),
            dma,
            dma((NG,)),
            dma,
            dma((NG, 2)),
            dma,
            dma((NG,)),
            dma,
            dma,
        ],
        compiler_params=pltpu.CompilerParams(
            collective_id=0, has_side_effects=True, vmem_limit_bytes=VMEM_LIMIT
        ),
        name="layer",
    )(*operands)


def shards(
    queries,
    key_vectors,
    value_vectors,
    log_decay,
    doc_ids,
    head_gain,
    output_weight,
    residual,
    norm_gain,
    routing,
    route_weights,
    gate_weight,
    up_weight,
    down_weight,
):
    return layer(
        queries,
        key_vectors,
        value_vectors,
        log_decay.T,
        doc_ids.reshape(1, -1),
        head_gain.reshape(1, -1),
        output_weight.T,
        residual,
        routing.T,
        route_weights.T,
        norm_gain.reshape(1, -1),
        gate_weight[0].T,
        up_weight[0].T,
        down_weight[0],
    )


def solution(mesh):
    in_specs = (
        P("seq", "head"),
        P("seq", "head"),
        P("seq", "head"),
        P("seq", "head"),
        P("seq"),
        P("head"),
        P("head", "seq"),
        P("seq", "head"),
        P(),
        P("seq", None),
        P("seq", None),
        P("seq", None, "head"),
        P("seq", None, "head"),
        P("seq", "head", None),
    )
    return jax.shard_map(
        shards, mesh=mesh, in_specs=in_specs, out_specs=P("seq", "head"), check_vma=False
    )
```
